32 devices in a mesh: dp: 4 (over y, core), tensor: 8 (over z, x).
Axes of the slice: x: 2, y: 2, z: 4, core: 2. Of those that a mesh axis runs over, the one named last changes fastest.
Arguments:
- tokens: bfloat16 [8192, 2048], P(('dp', 'tensor')), may hold values from -6 to 6
- gain_one: float32 [2048], replicated, may hold values from 0.5 to 1.5
- w_query: bfloat16 [2048, 256], P(None, 'tensor'), may hold values from -0.125 to 0.125
- w_key: bfloat16 [2048, 256], P(None, 'tensor'), may hold values from -0.125 to 0.125
- w_value: bfloat16 [2048, 2048], P(None, 'tensor'), may hold values from -0.125 to 0.125
- w_out: bfloat16 [2048, 2048], P('tensor'), may hold values from -0.5 to 0.5
- gain_two: float32 [2048], replicated, may hold values from 0.5 to 1.5
- w_gate: bfloat16 [2048, 5632], P(None, 'tensor'), may hold values from -0.125 to 0.125
- w_up: bfloat16 [2048, 5632], P(None, 'tensor'), may hold values from -0.125 to 0.125
- w_down: bfloat16 [5632, 2048], P('tensor'), may hold values from -0.078125 to 0.078125
- doc_ids: int32 [4, 2048], P('dp'), may hold values from 0 to 7, never falling along the last dimension, each value on 1 to 1024 neighbouring positions
- cotangent: bfloat16 [8192, 2048], P(('dp', 'tensor')), may hold values from -6 to 6
Outputs:
- block_out: bfloat16 [8192, 2048], P(('dp', 'tensor'))
- grad_tokens: float32 [8192, 2048], P(('dp', 'tensor'))
- grad_gain_one: float32 [2048], replicated
- grad_query: float32 [2048, 256], P(None, 'tensor')
- grad_key: float32 [2048, 256], P(None, 'tensor')
- grad_value: float32 [2048, 2048], P(None, 'tensor')
- grad_out_proj: float32 [2048, 2048], P('tensor')
- grad_gain_two: float32 [2048], replicated
- grad_gate: float32 [2048, 5632], P(None, 'tensor')
- grad_up: float32 [2048, 5632], P(None, 'tensor')
- grad_down: float32 [5632, 2048], P('tensor')
The draws below stay inside these ranges and needn't reach their ends.
Inputs may be any that keep to these rules, and one draw needn't show every extreme that they name: Each row of doc_ids never falls along the row; each of the 8 documents of a group has 1 to 1024 tokens, and one has exactly 1024.
All inputs are finite; a program needn't handle non-finite values.
Results may differ from the reference program's by a relative error of at most 0.02.
Values may be sent and summed in bfloat16 or wider, within the bound.
No kernel may reach another device: no remote copies, remote signals or barrier semaphores. Data moves between devices by JAX's collectives and lax.ppermute only.
A program may use at most 256 MiB of HBM per device.

```python
import math
import jax
import jax.numpy as jnp
import numpy as np
from jax import lax

D = 2048
HEADS = 16
FEAT = 16
FF = 5632
SEQS = 8
HEAD_V = 128
GROUP_TOK = 2048
MAX_LEN = 1024
TOKENS = 8192
BLOCK = 512
N_DP = 4


def steps_of(own_key, dims, cuts, low, largest):
    def one(position, blocks):
        steps = jax.random.uniform(jax.random.fold_in(jax.random.fold_in(own_key, 6), position), (blocks,), jnp.float32, low / len(cuts), largest / len(cuts))
        return jnp.repeat(jnp.exp(steps), dims[position] // blocks).reshape((-1,) + (1,) * (len(dims) - position - 1))

    loudness = one(*cuts[0])
    for cut in cuts[1:]:
        loudness = loudness * one(*cut)
    return loudness


def profile(count, total, limit, skew):
    weights = [(1 << 20) // math.isqrt(grade ** skew) + 1 for grade in range(2, count + 1)]
    rest, holding = total - limit - (count - 1), [1] * (count - 1)
    while rest > 0:
        free = [i for i in range(count - 1) if holding[i] < limit]
        whole, budget = sum([weights[i] for i in free]), rest
        for i in free:
            more = min(limit - holding[i], max(1, budget * weights[i] // whole), rest)
            holding[i] = holding[i] + more
            rest = rest - more
    return np.array([limit] + holding)


def uneven_parts(rng, amount, total, most, slope):
    if amount == 2:
        one = jax.random.randint(rng, (), max(1, total - most), min(most, total - 1) + 1)
        return jnp.stack([one, total - one])
    tallies = jnp.asarray(profile(amount, total, most, slope), jnp.int32)
    twos = (amount - 1) // 2
    giver, sink = tallies[1:1 + 2 * twos:2], tallies[2:2 + 2 * twos:2]
    margin = jnp.minimum(giver - 1, most - sink)
    shifted = jax.random.randint(jax.random.fold_in(rng, 1), (twos,), 0, 1 << 20) % (margin + 1)
    tallies = tallies.at[1:1 + 2 * twos:2].set(giver - shifted).at[2:2 + 2 * twos:2].set(sink + shifted)
    return tallies[jax.random.permutation(jax.random.fold_in(rng, 2), amount)]


def scatter_about(stream_key, dims, width, limit, split=(), held_as=jnp.bfloat16):
    loudness = steps_of(stream_key, dims, split, -0.22, 0.18) if split else 1.0
    entries = jax.random.normal(stream_key, dims, jnp.float32) * width * loudness
    return jnp.minimum(jnp.maximum(entries, -limit), limit).astype(held_as)


def setup_inputs(seed: int = 0) -> dict:
    key_list = jax.random.split(jax.random.key(seed), 13)
    return {
        "tokens": scatter_about(key_list[0], (TOKENS, D), 1.0, 6.0, ((0, 32),)),
        "gain_one": jnp.clip(1.0 + 0.1 * jax.random.normal(key_list[1], (D,), jnp.float32), 0.5, 1.5),
        "w_query": scatter_about(key_list[2], (D, HEADS * FEAT), D ** -0.5, 0.125, ((1, 8),)),
        "w_key": scatter_about(key_list[3], (D, HEADS * FEAT), D ** -0.5, 0.125, ((1, 8),)),
        "w_value": scatter_about(key_list[4], (D, D), D ** -0.5, 0.125, ((1, 8),)),
        "w_out": scatter_about(key_list[5], (D, D), (D // 16) ** -0.5, 0.5, ((0, 8),)),
        "gain_two": jnp.clip(1.0 + 0.1 * jax.random.normal(key_list[6], (D,), jnp.float32), 0.5, 1.5),
        "w_gate": scatter_about(key_list[7], (D, FF), D ** -0.5, 0.125, ((1, 8),)),
        "w_up": scatter_about(key_list[8], (D, FF), D ** -0.5, 0.125, ((1, 8),)),
        "w_down": scatter_about(key_list[9], (FF, D), FF ** -0.5, 0.078125, ((0, 8),)),
        "doc_ids": jax.vmap(lambda own: jnp.searchsorted(jnp.cumsum(uneven_parts(own, SEQS, GROUP_TOK, MAX_LEN, 2)), jnp.arange(GROUP_TOK), side="right"))(jax.random.split(key_list[10], N_DP)).reshape((N_DP, GROUP_TOK)).astype(jnp.int32),
        "cotangent": scatter_about(key_list[11], (TOKENS, D), 1.0, 6.0, ((0, 32),)),
    }


@jax.custom_vjp
def low(v):
    return lax.optimization_barrier(v.astype(jnp.bfloat16)).astype(jnp.float32)

@jax.custom_vjp
def lower_backward(v):
    return v

def low_keep(v):
    return (low(v), None)

def low_pass(kept, grad):
    return (grad,)

def back_keep(v):
    return (v, None)

def back_low(kept, grad):
    return (low(grad),)
low.defvjp(low_keep, low_pass)
lower_backward.defvjp(back_keep, back_low)
EPS = 1e-05
HIGH_PRECISION = lax.Precision.HIGHEST

def rms_norm(values, gain_vec):
    row_scale = lax.rsqrt(lax.optimization_barrier(jnp.mean(values * values, axis=-1, keepdims=True)) + EPS)
    return values * row_scale * gain_vec

def taylor_attention(query_rows, key_row_block, value_rows, doc_row):
    block_count = GROUP_TOK // BLOCK
    query_blocks = query_rows.reshape(block_count, BLOCK, HEADS, FEAT)
    every_key_row = key_row_block.reshape(GROUP_TOK, HEADS, FEAT)
    values_all = value_rows.reshape(GROUP_TOK, HEADS, HEAD_V)
    positions = jnp.arange(GROUP_TOK, dtype=jnp.int32)
    doc_blocks = doc_row.reshape(block_count, BLOCK)
    pos_blocks = positions.reshape(block_count, BLOCK)

    def one_block(items):
        query_portion, doc_part, pos_part = items
        score_matrix = lower_backward(jnp.einsum('gsn,jsn->sgj', query_portion, every_key_row, precision=HIGH_PRECISION) * 0.25)
        allowed = (doc_part[:, None] == doc_row[None, :]) & (pos_part[:, None] >= positions[None, :])
        kernel = jnp.where(allowed[None], 1.0 + score_matrix + 0.5 * score_matrix * score_matrix, 0.0)
        denominator = lax.optimization_barrier(jnp.sum(kernel, axis=-1))
        numerator = lower_backward(jnp.einsum('hqk,khd->qhd', low(kernel), values_all, precision=HIGH_PRECISION))
        return numerator / denominator.T[:, :, None]
    mixed_heads = lax.map(jax.checkpoint(one_block), (query_blocks, doc_blocks, pos_blocks))
    return mixed_heads.reshape(GROUP_TOK, HEADS * HEAD_V)

def layer(inputs, weights, doc_row):
    gain_one, w_query, w_key, w_value, w_out, gain_two, w_gate, w_up, w_down = weights
    first = low(rms_norm(inputs, gain_one))
    query_rows = lower_backward(low(jnp.dot(first, w_query, precision=HIGH_PRECISION)))
    key_row_block = lower_backward(low(jnp.dot(first, w_key, precision=HIGH_PRECISION)))
    value_rows = lower_backward(low(jnp.dot(first, w_value, precision=HIGH_PRECISION)))
    mixed_heads = lower_backward(low(taylor_attention(query_rows, key_row_block, value_rows, doc_row)))
    attn_out = lower_backward(jnp.dot(mixed_heads, w_out, precision=HIGH_PRECISION))
    residual = inputs + attn_out
    second = low(rms_norm(residual, gain_two))
    gate_pre = lower_backward(jnp.dot(second, w_gate, precision=HIGH_PRECISION))
    upward = lower_backward(jnp.dot(second, w_up, precision=HIGH_PRECISION))
    hidden = low(jax.nn.silu(gate_pre) * upward)
    return residual + jnp.dot(hidden, w_down, precision=HIGH_PRECISION)

def reference(tokens, gain_one, w_query, w_key, w_value, w_out, gain_two, w_gate, w_up, w_down, doc_ids, cotangent):
    params = (gain_one, w_query.astype(jnp.float32), w_key.astype(jnp.float32), w_value.astype(jnp.float32), w_out.astype(jnp.float32), gain_two, w_gate.astype(jnp.float32), w_up.astype(jnp.float32), w_down.astype(jnp.float32))
    inputs = tokens.astype(jnp.float32).reshape(N_DP, GROUP_TOK, D)
    grads_in = cotangent.astype(jnp.float32).reshape(N_DP, GROUP_TOK, D)
    zeros = jax.tree.map(jnp.zeros_like, params)

    def per_group(totals, items):
        group_in, group_grad, group_docs = items

        def forward(values_in, weights):
            return layer(values_in, weights, group_docs)
        result, pull = jax.vjp(forward, group_in, params)
        grad_in, grad_weights = pull(group_grad)
        totals = jax.tree.map(lambda left, right: left + right, totals, grad_weights)
        return (totals, (result.astype(jnp.bfloat16), grad_in))
    totals, (outputs, grad_inputs) = lax.scan(per_group, zeros, (inputs, grads_in, doc_ids))
    return (outputs.reshape(TOKENS, D), grad_inputs.reshape(TOKENS, D), totals[0], totals[1], totals[2], totals[3], totals[4], totals[5], totals[6], totals[7], totals[8])
```

```python
import jax
import jax.numpy as jnp
from jax import lax
from jax.sharding import Mesh
from jax.sharding import PartitionSpec as P

FEAT = 16
HEAD_V = 128
EPS = 1e-05

ALL_AXES = ("y", "k", "h", "l", "x")
SQUARE = ("k", "l", "x")


def norm_rows(values, gain_vec):
    row_scale = lax.rsqrt(jnp.mean(values * values, axis=-1, keepdims=True) + EPS)
    normed = values * row_scale
    return (normed, row_scale, (normed * gain_vec).astype(jnp.bfloat16))


def norm_back(grad_normed, normed, row_scale, gain_vec):
    weighted = grad_normed * gain_vec
    inner_mean = jnp.mean(weighted * normed, axis=-1, keepdims=True)
    return row_scale * (weighted - normed * inner_mean)


def dot_nn(left_mat, right_mat):
    return jnp.dot(left_mat, right_mat, preferred_element_type=jnp.float32)


def dot_tn(left_mat, right_mat):
    return lax.dot_general(
        left_mat, right_mat, (((0,), (0,)), ((), ())), preferred_element_type=jnp.float32
    )


def dot_nt(left_mat, right_mat):
    return lax.dot_general(
        left_mat, right_mat, (((1,), (1,)), ((), ())), preferred_element_type=jnp.float32
    )


def block_kernel(query_rows, key_row_block, doc_row, row_start, block_rows):
    row_end_index = row_start + block_rows
    query_portion = query_rows[row_start:row_end_index]
    score_matrix = (
        jnp.einsum(
            "gsn,jsn->sgj",
            query_portion,
            key_row_block[:row_end_index],
            preferred_element_type=jnp.float32,
        )
        * 0.25
    )
    query_index = row_start + jnp.arange(block_rows)
    key_index = jnp.arange(row_end_index)
    allowed = (doc_row[row_start:row_end_index, None] == doc_row[None, :row_end_index]) & (
        query_index[:, None] >= key_index[None, :]
    )
    kernel = jnp.where(allowed[None], 1.0 + score_matrix + 0.5 * score_matrix * score_matrix, 0.0)
    return (score_matrix, allowed, kernel)


def attention_forward(query_rows, key_row_block, value_rows, doc_row, block_rows):
    group_rows = query_rows.shape[0]
    outputs = []
    denoms = []
    for row_start in range(0, group_rows, block_rows):
        row_end_index = row_start + block_rows
        score_matrix, allowed, kernel = block_kernel(
            query_rows, key_row_block, doc_row, row_start, block_rows
        )
        denominator = jnp.sum(kernel, axis=-1)
        numerator = jnp.einsum(
            "hqk,khd->qhd",
            kernel.astype(jnp.bfloat16),
            value_rows[:row_end_index],
            preferred_element_type=jnp.float32,
        )
        outputs.append((numerator / denominator.T[:, :, None]).astype(jnp.bfloat16))
        denoms.append(denominator)
    return (jnp.concatenate(outputs, axis=0), jnp.concatenate(denoms, axis=1))


def attention_backward(
    query_rows, key_row_block, value_rows, doc_row, denoms, grad_mixed, block_rows
):
    group_rows = query_rows.shape[0]
    grad_queries = []
    grad_keys = jnp.zeros(key_row_block.shape, jnp.float32)
    grad_values = jnp.zeros(value_rows.shape, jnp.float32)
    for row_start in range(0, group_rows, block_rows):
        row_end_index = row_start + block_rows
        score_matrix, allowed, kernel = block_kernel(
            query_rows, key_row_block, doc_row, row_start, block_rows
        )
        kernel_low = kernel.astype(jnp.bfloat16)
        denominator = denoms[:, row_start:row_end_index]
        numerator = jnp.einsum(
            "hqk,khd->qhd",
            kernel_low,
            value_rows[:row_end_index],
            preferred_element_type=jnp.float32,
        )
        grad_output = grad_mixed[row_start:row_end_index].astype(jnp.float32)
        grad_numer = (grad_output / denominator.T[:, :, None]).astype(jnp.bfloat16)
        grad_denom = -jnp.sum(grad_output * numerator, axis=-1).T / (denominator * denominator)
        grad_kernel = (
            jnp.einsum(
                "qhd,khd->hqk",
                grad_numer,
                value_rows[:row_end_index],
                preferred_element_type=jnp.float32,
            )
            + grad_denom[:, :, None]
        )
        score_gradients = jnp.where(allowed[None], grad_kernel * (1.0 + score_matrix), 0.0).astype(
            jnp.bfloat16
        )
        grad_queries.append(
            jnp.einsum(
                "zxu,uzc->xzc",
                score_gradients,
                key_row_block[:row_end_index],
                preferred_element_type=jnp.float32,
            )
            * 0.25
        )
        grad_keys = grad_keys.at[:row_end_index].add(
            jnp.einsum(
                "ari,ran->ian",
                score_gradients,
                query_rows[row_start:row_end_index],
                preferred_element_type=jnp.float32,
            )
            * 0.25
        )
        grad_values = grad_values.at[:row_end_index].add(
            jnp.einsum("hqk,qhd->khd", kernel_low, grad_numer, preferred_element_type=jnp.float32)
        )
    grad_query_rows = jnp.concatenate(grad_queries, axis=0).astype(jnp.bfloat16)
    return (grad_query_rows, grad_keys.astype(jnp.bfloat16), grad_values.astype(jnp.bfloat16))


def make_body(y_size):
    y_pairs = [(i, i ^ 1) for i in range(y_size)]

    def trade(values):
        return lax.ppermute(values, ("k", "h"), [(0, 0), (1, 2), (2, 1), (3, 3)])

    def over_y(values):
        return lax.ppermute(values, "y", y_pairs)

    def fetch_shard(own, axis):
        half = own.shape[axis] // 2
        mine = lax.dynamic_slice_in_dim(own, (lax.axis_index("y") % 2) * half, half, axis)
        got = trade(mine)
        other = over_y(got)
        return jnp.concatenate([got, other], axis=axis)

    def reduce_grad(part, axis):
        half = part.shape[axis] // 2
        mine = lax.slice_in_dim(part, 0, half, axis=axis)
        other = lax.slice_in_dim(part, half, 2 * half, axis=axis)
        total = mine + over_y(other)
        step = 2
        while step < y_size:
            total = total + lax.ppermute(total, "y", [(i, i ^ step) for i in range(y_size)])
            step *= 2
        arrived = lax.ppermute(total, ("k", "h"), [(1, 0), (2, 3)])
        total = total + arrived
        twin = lax.ppermute(total, ("k", "h"), [(0, 2), (3, 1)])
        mine = jnp.where(lax.axis_index("k") == lax.axis_index("h"), total, twin)
        other = over_y(mine)
        first = lax.axis_index("y") % 2 == 0
        return jnp.where(
            first,
            jnp.concatenate([mine, other], axis=axis),
            jnp.concatenate([other, mine], axis=axis),
        ).astype(jnp.float32)

    def gather(rows):
        return lax.all_gather(rows, SQUARE, axis=0, tiled=True)

    def scatter(parts):
        return lax.psum_scatter(parts, SQUARE, scatter_dimension=0, tiled=True)

    def body(
        tokens,
        gain_one,
        w_query,
        w_key,
        w_value,
        w_out,
        gain_two,
        w_gate,
        w_up,
        w_down,
        doc_ids,
        cotangent,
    ):
        doc_row = trade(doc_ids)[0]
        own_tokens = trade(tokens)
        inputs = own_tokens.astype(jnp.float32)
        own_grad = trade(cotangent)
        wq = fetch_shard(w_query.T, 0)
        wk = fetch_shard(w_key.T, 0)
        wv = fetch_shard(w_value, 1)
        wo = fetch_shard(w_out, 0)
        wg = fetch_shard(w_gate.T, 0)
        wu = fetch_shard(w_up.T, 0)
        wd = fetch_shard(w_down, 0)
        heads_here = wq.shape[0] // FEAT
        wqk = jnp.concatenate([wq, wk], axis=0)

        normed_one, scale_one, low_one = norm_rows(inputs, gain_one)
        gathered_one = gather(low_one)
        group_rows = gathered_one.shape[0]
        block_rows = min(512, group_rows)
        qk_flat = dot_nt(gathered_one, wqk).astype(jnp.bfloat16)
        value_flat = dot_nn(gathered_one, wv).astype(jnp.bfloat16)
        width = heads_here * FEAT
        query_rows = qk_flat[:, :width].reshape(group_rows, heads_here, FEAT)
        key_row_block = qk_flat[:, width:].reshape(group_rows, heads_here, FEAT)
        value_rows = value_flat.reshape(group_rows, heads_here, HEAD_V)
        mixed_blocks, denoms = attention_forward(
            query_rows, key_row_block, value_rows, doc_row, block_rows
        )
        mixed_heads = mixed_blocks.reshape(group_rows, heads_here * HEAD_V)
        attn_out = scatter(dot_nn(mixed_heads, wo).astype(jnp.bfloat16)).astype(jnp.float32)
        residual = inputs + attn_out
        normed_two, scale_two, low_two = norm_rows(residual, gain_two)
        grad_rows = gather(own_grad)
        gathered_two = gather(low_two)
        gate_pre = dot_nt(gathered_two, wg)
        upward = dot_nt(gathered_two, wu)
        sigmoid_gate = jax.nn.sigmoid(gate_pre)
        hidden = (gate_pre * sigmoid_gate * upward).astype(jnp.bfloat16)
        grad_hidden = dot_nt(grad_rows, wd)
        slope_gate = sigmoid_gate * (1.0 + gate_pre * (1.0 - sigmoid_gate))
        grad_gate_act = (grad_hidden * upward * slope_gate).astype(jnp.bfloat16)
        grad_upward = (grad_hidden * (gate_pre * sigmoid_gate)).astype(jnp.bfloat16)
        grad_normed_two = scatter(
            (dot_nn(grad_gate_act, wg) + dot_nn(grad_upward, wu)).astype(jnp.bfloat16)
        ).astype(jnp.float32)
        grad_gate_w = dot_tn(grad_gate_act, gathered_two).astype(jnp.bfloat16)
        grad_up_w = dot_tn(grad_upward, gathered_two).astype(jnp.bfloat16)
        grad_down_w = dot_tn(hidden, grad_rows).astype(jnp.bfloat16)
        ffn_out = scatter(dot_nn(hidden, wd).astype(jnp.bfloat16)).astype(jnp.float32)
        block_out = trade((residual + ffn_out).astype(jnp.bfloat16))

        gain_two_part = jnp.sum(grad_normed_two * normed_two, axis=0)
        grad_resid = own_grad.astype(jnp.float32) + norm_back(
            grad_normed_two, normed_two, scale_two, gain_two
        )
        grad_attn_rows = gather(grad_resid.astype(jnp.bfloat16))
        grad_mixed = dot_nt(grad_attn_rows, wo).astype(jnp.bfloat16)
        grad_out_w = dot_tn(mixed_heads, grad_attn_rows).astype(jnp.bfloat16)
        grad_query_rows, grad_key_rows, grad_value_rows = attention_backward(
            query_rows,
            key_row_block,
            value_rows,
            doc_row,
            denoms,
            grad_mixed.reshape(group_rows, heads_here, HEAD_V),
            block_rows,
        )
        grad_qk_flat = jnp.concatenate(
            [grad_query_rows.reshape(group_rows, -1), grad_key_rows.reshape(group_rows, -1)],
            axis=1,
        )
        grad_value_flat = grad_value_rows.reshape(group_rows, heads_here * HEAD_V)
        grad_normed_one = scatter(
            (dot_nn(grad_qk_flat, wqk) + dot_nt(grad_value_flat, wv)).astype(jnp.bfloat16)
        ).astype(jnp.float32)
        grad_qk_w = dot_tn(grad_qk_flat, gathered_one)
        grad_value_w = dot_tn(gathered_one, grad_value_flat)
        gain_one_part = (
            jnp.sum(grad_qk_w * wqk, axis=0) + jnp.sum(grad_value_w * wv, axis=1)
        ) / gain_one
        grad_tokens = grad_resid + norm_back(grad_normed_one, normed_one, scale_one, gain_one)
        grad_tokens = trade(grad_tokens.astype(jnp.bfloat16)).astype(jnp.float32)
        gain_parts = lax.all_gather(jnp.stack([gain_one_part, gain_two_part]), ALL_AXES)
        gain_grads = jnp.sum(gain_parts, axis=0)
        grad_qk_w = grad_qk_w.astype(jnp.bfloat16)
        grad_query_w = reduce_grad(grad_qk_w[:width], 0)
        grad_key_w = reduce_grad(grad_qk_w[width:], 0)
        return (
            block_out,
            grad_tokens,
            gain_grads[0],
            grad_query_w.T,
            grad_key_w.T,
            reduce_grad(grad_value_w.astype(jnp.bfloat16), 1),
            reduce_grad(grad_out_w, 0),
            gain_grads[1],
            reduce_grad(grad_gate_w, 0).T,
            reduce_grad(grad_up_w, 0).T,
            reduce_grad(grad_down_w, 0),
        )

    return body


def solution(mesh):
    dp_size, tensor_size = mesh.devices.shape
    fine = Mesh(mesh.devices.reshape(dp_size // 2, 2, 2, 2, tensor_size // 4), ALL_AXES)
    rows = P(ALL_AXES, None)
    shard = ("h", "l", "x")
    in_specs = (
        rows,
        P(),
        P(None, shard),
        P(None, shard),
        P(None, shard),
        P(shard, None),
        P(),
        P(None, shard),
        P(None, shard),
        P(shard, None),
        P(("y", "k"), None),
        rows,
    )
    out_specs = (
        rows,
        rows,
        P(),
        P(None, shard),
        P(None, shard),
        P(None, shard),
        P(shard, None),
        P(),
        P(None, shard),
        P(None, shard),
        P(shard, None),
    )
    return jax.shard_map(
        make_body(dp_size // 2), mesh=fine, in_specs=in_specs, out_specs=out_specs, check_vma=False
    )
```

```python
import jax
import jax.numpy as jnp
from jax import lax
from jax.sharding import Mesh
from jax.sharding import PartitionSpec as P

FEAT = 16
HEAD_V = 128
EPS = 1e-05

ALL_AXES = ("y", "k", "h", "l", "x")
FLIP = [(0, 1), (1, 0)]
SQUARE = ("k", "l", "x")


def norm_rows(values, gain_vec):
    row_scale = lax.rsqrt(jnp.mean(values * values, axis=-1, keepdims=True) + EPS)
    normed = values * row_scale
    return (normed, row_scale, (normed * gain_vec).astype(jnp.bfloat16))


def norm_back(grad_normed, normed, row_scale, gain_vec):
    weighted = grad_normed * gain_vec
    inner_mean = jnp.mean(weighted * normed, axis=-1, keepdims=True)
    return row_scale * (weighted - normed * inner_mean)


def dot_nn(left_mat, right_mat):
    return jnp.dot(left_mat, right_mat, preferred_element_type=jnp.float32)


def dot_tn(left_mat, right_mat):
    return lax.dot_general(
        left_mat, right_mat, (((0,), (0,)), ((), ())), preferred_element_type=jnp.float32
    )


def dot_nt(left_mat, right_mat):
    return lax.dot_general(
        left_mat, right_mat, (((1,), (1,)), ((), ())), preferred_element_type=jnp.float32
    )


def block_kernel(query_rows, key_row_block, doc_row, row_start, block_rows):
    row_end_index = row_start + block_rows
    query_portion = query_rows[row_start:row_end_index]
    score_matrix = (
        jnp.einsum(
            "gsn,jsn->sgj",
            query_portion,
            key_row_block[:row_end_index],
            preferred_element_type=jnp.float32,
        )
        * 0.25
    )
    query_index = row_start + jnp.arange(block_rows)
    key_index = jnp.arange(row_end_index)
    allowed = (doc_row[row_start:row_end_index, None] == doc_row[None, :row_end_index]) & (
        query_index[:, None] >= key_index[None, :]
    )
    kernel = jnp.where(allowed[None], 1.0 + score_matrix + 0.5 * score_matrix * score_matrix, 0.0)
    return (score_matrix, allowed, kernel)


def attention_forward(query_rows, key_row_block, value_rows, doc_row, block_rows):
    group_rows = query_rows.shape[0]
    outputs = []
    denoms = []
    for row_start in range(0, group_rows, block_rows):
        row_end_index = row_start + block_rows
        score_matrix, allowed, kernel = block_kernel(
            query_rows, key_row_block, doc_row, row_start, block_rows
        )
        denominator = jnp.sum(kernel, axis=-1)
        numerator = jnp.einsum(
            "hqk,khd->qhd",
            kernel.astype(jnp.bfloat16),
            value_rows[:row_end_index],
            preferred_element_type=jnp.float32,
        )
        outputs.append((numerator / denominator.T[:, :, None]).astype(jnp.bfloat16))
        denoms.append(denominator)
    return (jnp.concatenate(outputs, axis=0), jnp.concatenate(denoms, axis=1))


def attention_backward(
    query_rows, key_row_block, value_rows, doc_row, denoms, grad_mixed, block_rows
):
    group_rows = query_rows.shape[0]
    grad_queries = []
    grad_keys = jnp.zeros(key_row_block.shape, jnp.float32)
    grad_values = jnp.zeros(value_rows.shape, jnp.float32)
    for row_start in range(0, group_rows, block_rows):
        row_end_index = row_start + block_rows
        score_matrix, allowed, kernel = block_kernel(
            query_rows, key_row_block, doc_row, row_start, block_rows
        )
        kernel_low = kernel.astype(jnp.bfloat16)
        denominator = denoms[:, row_start:row_end_index]
        numerator = jnp.einsum(
            "hqk,khd->qhd",
            kernel_low,
            value_rows[:row_end_index],
            preferred_element_type=jnp.float32,
        )
        grad_output = grad_mixed[row_start:row_end_index].astype(jnp.float32)
        grad_numer = (grad_output / denominator.T[:, :, None]).astype(jnp.bfloat16)
        grad_denom = -jnp.sum(grad_output * numerator, axis=-1).T / (denominator * denominator)
        grad_kernel = (
            jnp.einsum(
                "qhd,khd->hqk",
                grad_numer,
                value_rows[:row_end_index],
                preferred_element_type=jnp.float32,
            )
            + grad_denom[:, :, None]
        )
        score_gradients = jnp.where(allowed[None], grad_kernel * (1.0 + score_matrix), 0.0).astype(
            jnp.bfloat16
        )
        grad_queries.append(
            jnp.einsum(
                "zxu,uzc->xzc",
                score_gradients,
                key_row_block[:row_end_index],
                preferred_element_type=jnp.float32,
            )
            * 0.25
        )
        grad_keys = grad_keys.at[:row_end_index].add(
            jnp.einsum(
                "ari,ran->ian",
                score_gradients,
                query_rows[row_start:row_end_index],
                preferred_element_type=jnp.float32,
            )
            * 0.25
        )
        grad_values = grad_values.at[:row_end_index].add(
            jnp.einsum("hqk,qhd->khd", kernel_low, grad_numer, preferred_element_type=jnp.float32)
        )
    grad_query_rows = jnp.concatenate(grad_queries, axis=0).astype(jnp.bfloat16)
    return (grad_query_rows, grad_keys.astype(jnp.bfloat16), grad_values.astype(jnp.bfloat16))


def after(value, *others):
    return lax.optimization_barrier((value, *others))[0]


def make_body(y_size):
    y_pairs = [(i, i ^ 1) for i in range(y_size)]
    owner_y_pairs = [
        (i * 4 + kh, (i ^ 1) * 4 + kh) for i in range(y_size) for kh in (0, 3)
    ]

    def trade(values):
        return lax.ppermute(values, ("k", "h"), [(0, 0), (1, 2), (2, 1), (3, 3)])

    def over_y(values):
        return lax.ppermute(values, "y", y_pairs)

    def my_half(own, axis=0):
        half = own.shape[axis] // 2
        return lax.dynamic_slice_in_dim(own, (lax.axis_index("y") % 2) * half, half, axis)

    def scatter(lhs, product):
        k, l, x = (lax.axis_index(name) for name in SQUARE)
        blocks = lhs.reshape(2, 4, lhs.shape[0] // 8, lhs.shape[1])
        rows = lhs.shape[0] // 8
        half = rows // 2
        for_twin = lax.dynamic_index_in_dim(blocks, 1 - k, 0, keepdims=False)
        for_twin = product(for_twin.reshape(4 * rows, -1)).astype(jnp.bfloat16)
        from_twin = lax.ppermute(for_twin, "k", FLIP).reshape(4, rows, -1)
        mine = lax.dynamic_index_in_dim(blocks, k, 0, keepdims=False)

        def block(dl, dx):
            index = (l ^ dl) * 2 + (x ^ dx)
            part = product(lax.dynamic_index_in_dim(mine, index, 0, keepdims=False))
            return part + lax.dynamic_index_in_dim(from_twin, index, 0, keepdims=False)

        diagonal = block(1, 1).astype(jnp.bfloat16)
        along_x = block(0, 1)
        along_l = block(1, 0)
        got_top = lax.ppermute(diagonal[:half], "x", FLIP)
        got_bottom = lax.ppermute(diagonal[half:], "l", FLIP)
        x_top = lax.ppermute(along_x[:half].astype(jnp.bfloat16), "x", FLIP)
        l_bottom = lax.ppermute(along_l[half:].astype(jnp.bfloat16), "l", FLIP)
        own = block(0, 0)
        x_bottom = lax.ppermute((along_x[half:] + got_bottom).astype(jnp.bfloat16), "x", FLIP)
        l_top = lax.ppermute((along_l[:half] + got_top).astype(jnp.bfloat16), "l", FLIP)
        top = own[:half] + x_top + l_top
        bottom = own[half:] + x_bottom + l_bottom
        return jnp.concatenate([top, bottom], axis=0)

    def reduce_grad(other, mine_product):
        total = (mine_product() + over_y(other)).astype(jnp.bfloat16)
        y_total = total
        step = 2
        while step < y_size:
            total = total + lax.ppermute(total, "y", [(i, i ^ step) for i in range(y_size)])
            step *= 2
        total = total + lax.ppermute(total, ("k", "h"), [(1, 0), (2, 3)])
        back = lax.ppermute(total, ("y", "k", "h"), owner_y_pairs)
        to_twin = [(0, 2), (3, 1)]
        owner = lax.axis_index("k") == lax.axis_index("h")
        mine = jnp.where(owner, total, lax.ppermute(total, ("k", "h"), to_twin))
        theirs = jnp.where(owner, back, lax.ppermute(back, ("k", "h"), to_twin))
        return y_total, mine, theirs

    def in_order(mine, theirs, axis=0):
        first = lax.axis_index("y") % 2 == 0
        return jnp.where(
            first,
            jnp.concatenate([mine, theirs], axis=axis),
            jnp.concatenate([theirs, mine], axis=axis),
        ).astype(jnp.float32)

    def gather(rows):
        return lax.all_gather(rows, SQUARE, axis=0, tiled=True)

    def body(
        tokens,
        gain_one,
        w_query,
        w_key,
        w_value,
        w_out,
        gain_two,
        w_gate,
        w_up,
        w_down,
        doc_ids,
        cotangent,
    ):
        own_tokens = trade(tokens)
        doc_row = trade(doc_ids)[0]
        inputs = own_tokens.astype(jnp.float32)
        qkv_mine = trade(
            jnp.concatenate([my_half(w_value, 1).T, my_half(w_query.T), my_half(w_key.T)], axis=0)
        )
        qkv_other = over_y(qkv_mine)
        wide = qkv_mine.shape[0] - 2 * FEAT
        w_qkv = jnp.concatenate(
            [qkv_mine[:wide], qkv_other[:wide], qkv_mine[wide:], qkv_other[wide:]], axis=0
        )
        normed_one, scale_one, low_one = norm_rows(inputs, gain_one)
        gathered_one = gather(low_one)

        wo_half, gate_half, up_half, down_half, cotangent_in = lax.optimization_barrier(
            (
                my_half(w_out),
                my_half(w_gate.T),
                my_half(w_up.T),
                my_half(w_down),
                cotangent,
                own_tokens,
                qkv_mine,
            )
        )[:5]
        wo_mine = trade(wo_half)
        own_grad = trade(cotangent_in)
        down_mine = trade(down_half)
        gate_mine = trade(gate_half)
        up_mine = trade(up_half)

        def whole(mine):
            return jnp.concatenate([mine, over_y(mine)], axis=0)

        wo = whole(wo_mine)
        wd = whole(down_mine)
        wg = whole(gate_mine)
        wu = whole(up_mine)

        group_rows = gathered_one.shape[0]
        block_rows = min(512, group_rows)
        qkv = dot_nt(gathered_one, w_qkv).astype(jnp.bfloat16)
        value_rows = qkv[:, : 2 * HEAD_V].reshape(group_rows, 2, HEAD_V)
        small = qkv[:, 2 * HEAD_V :].reshape(group_rows, 2, 2, FEAT)
        query_rows = small[:, :, 0]
        key_row_block = small[:, :, 1]
        mixed_blocks, denoms = attention_forward(
            query_rows, key_row_block, value_rows, doc_row, block_rows
        )
        mixed_heads = mixed_blocks.reshape(group_rows, 2 * HEAD_V)
        grad_rows = gather(own_grad)
        attn_out = scatter(mixed_heads, lambda rows: dot_nn(rows, wo))
        residual = inputs + attn_out
        normed_two, scale_two, low_two = norm_rows(residual, gain_two)
        gathered_two = gather(low_two)
        grad_hidden = dot_nt(grad_rows, wd)
        gate_pre = dot_nt(gathered_two, wg)
        upward = dot_nt(gathered_two, wu)
        sigmoid_gate = jax.nn.sigmoid(gate_pre)
        hidden = (gate_pre * sigmoid_gate * upward).astype(jnp.bfloat16)
        slope_gate = sigmoid_gate * (1.0 + gate_pre * (1.0 - sigmoid_gate))
        grad_gate_act = (grad_hidden * upward * slope_gate).astype(jnp.bfloat16)
        grad_upward = (grad_hidden * (gate_pre * sigmoid_gate)).astype(jnp.bfloat16)
        width = grad_upward.shape[1]

        grad_normed_two = scatter(
            jnp.concatenate([grad_gate_act, grad_upward], axis=1),
            lambda rows: dot_nn(rows[:, :width], wg) + dot_nn(rows[:, width:], wu),
        )
        grads = {}
        half = width // 2
        for name, acts, rows in (
            ("gate", grad_gate_act, gathered_two),
            ("up", grad_upward, gathered_two),
            ("down", hidden, grad_rows),
        ):
            grads[name] = reduce_grad(
                dot_tn(acts[:, half:], rows).astype(jnp.bfloat16),
                lambda acts=acts, rows=rows: dot_tn(acts[:, :half], rows),
            )[1:]

        gain_two_part = jnp.sum(grad_normed_two * normed_two, axis=0)
        grad_resid = own_grad.astype(jnp.float32) + norm_back(
            grad_normed_two, normed_two, scale_two, gain_two
        )
        grad_attn_rows = gather(grad_resid.astype(jnp.bfloat16))
        ffn_out = scatter(hidden, lambda rows: dot_nn(rows, wd))
        block_out = trade((residual + ffn_out).astype(jnp.bfloat16))
        grad_mixed = dot_nt(grad_attn_rows, wo).astype(jnp.bfloat16)
        grads["out"] = reduce_grad(
            dot_tn(mixed_heads[:, HEAD_V:], grad_attn_rows).astype(jnp.bfloat16),
            lambda: dot_tn(mixed_heads[:, :HEAD_V], grad_attn_rows),
        )[1:]
        grad_query_rows, grad_key_rows, grad_value_rows = attention_backward(
            query_rows,
            key_row_block,
            value_rows,
            doc_row,
            denoms,
            grad_mixed.reshape(group_rows, 2, HEAD_V),
            block_rows,
        )
        halves = [
            jnp.concatenate(
                [grad_value_rows[:, i], grad_query_rows[:, i], grad_key_rows[:, i]], axis=1
            )
            for i in (0, 1)
        ]
        grad_normed_one = scatter(
            jnp.concatenate(halves, axis=1),
            lambda rows: dot_nn(rows[:, : rows.shape[1] // 2], qkv_mine)
            + dot_nn(rows[:, rows.shape[1] // 2 :], qkv_other),
        )
        qkv_y, qkv_grad_mine, qkv_grad_other = reduce_grad(
            dot_tn(halves[1], gathered_one).astype(jnp.bfloat16),
            lambda: dot_tn(halves[0], gathered_one),
        )
        gain_one_part = (
            jnp.sum(qkv_y.astype(jnp.float32) * qkv_mine.astype(jnp.float32), axis=0) / gain_one
        )
        gain_grads = jnp.stack([gain_one_part, gain_two_part])
        for name in ("k", "l", "x", "h"):
            gain_grads = gain_grads + lax.ppermute(gain_grads, name, FLIP)
        step = 1
        while step < y_size:
            gain_grads = gain_grads + lax.ppermute(
                gain_grads, "y", [(i, i ^ step) for i in range(y_size)]
            )
            step *= 2
        grad_tokens = grad_resid + norm_back(grad_normed_one, normed_one, scale_one, gain_one)
        grad_tokens = trade(grad_tokens.astype(jnp.bfloat16)).astype(jnp.float32)
        value_grad = in_order(qkv_grad_mine[:wide].T, qkv_grad_other[:wide].T, 1)
        query_grad = in_order(
            qkv_grad_mine[wide : wide + FEAT], qkv_grad_other[wide : wide + FEAT]
        ).T
        key_grad = in_order(qkv_grad_mine[wide + FEAT :], qkv_grad_other[wide + FEAT :]).T
        return (
            block_out,
            grad_tokens,
            gain_grads[0],
            query_grad,
            key_grad,
            value_grad,
            in_order(*grads["out"]),
            gain_grads[1],
            in_order(*grads["gate"]).T,
            in_order(*grads["up"]).T,
            in_order(*grads["down"]),
        )

    return body


def solution(mesh):
    dp_size, tensor_size = mesh.devices.shape
    fine = Mesh(mesh.devices.reshape(dp_size // 2, 2, 2, 2, tensor_size // 4), ALL_AXES)
    rows = P(ALL_AXES, None)
    shard = ("h", "l", "x")
    in_specs = (
        rows,
        P(),
        P(None, shard),
        P(None, shard),
        P(None, shard),
        P(shard, None),
        P(),
        P(None, shard),
        P(None, shard),
        P(shard, None),
        P(("y", "k"), None),
        rows,
    )
    out_specs = (
        rows,
        rows,
        P(),
        P(None, shard),
        P(None, shard),
        P(None, shard),
        P(shard, None),
        P(),
        P(None, shard),
        P(None, shard),
        P(shard, None),
    )
    return jax.shard_map(
        make_body(dp_size // 2), mesh=fine, in_specs=in_specs, out_specs=out_specs, check_vma=False
    )
```

```python
import functools

import jax
import jax.numpy as jnp
from jax import lax
from jax.experimental import pallas as pl
from jax.experimental.pallas import tpu as pltpu
from jax.sharding import Mesh
from jax.sharding import PartitionSpec as P

FEAT = 16
HEAD_V = 128
EPS = 1e-05
VALUES = 2 * HEAD_V
FEATS = 2 * FEAT
NO_COST = pl.CostEstimate(flops=1, bytes_accessed=1, transcendentals=0)

ALL_AXES = ("y", "k", "h", "l", "x")
FLIP = [(0, 1), (1, 0)]
SQUARE = ("k", "l", "x")


def norm_rows(values, gain_vec):
    row_scale = lax.rsqrt(jnp.mean(values * values, axis=-1, keepdims=True) + EPS)
    normed = values * row_scale
    return (normed, row_scale, (normed * gain_vec).astype(jnp.bfloat16))


def norm_back(grad_normed, normed, row_scale, gain_vec):
    weighted = grad_normed * gain_vec
    inner_mean = jnp.mean(weighted * normed, axis=-1, keepdims=True)
    return row_scale * (weighted - normed * inner_mean)


def dot_nn(left_mat, right_mat):
    return jnp.dot(left_mat, right_mat, preferred_element_type=jnp.float32)


def dot_tn(left_mat, right_mat):
    return lax.dot_general(
        left_mat, right_mat, (((0,), (0,)), ((), ())), preferred_element_type=jnp.float32
    )


def dot_nt(left_mat, right_mat):
    return lax.dot_general(
        left_mat, right_mat, (((1,), (1,)), ((), ())), preferred_element_type=jnp.float32
    )


def head_lanes(values, head):
    lane = lax.broadcasted_iota(jnp.int32, values.shape, 1)
    return jnp.where((lane >= head * FEAT) & (lane < (head + 1) * FEAT), values, jnp.zeros_like(values))

def scores(query, keys, ends_ref, i, j, block):
    score = dot_nt(query, keys) * 0.25
    t = i * block + lax.broadcasted_iota(jnp.int32, score.shape, 0)
    u = j * block + lax.broadcasted_iota(jnp.int32, score.shape, 1)
    ends = ends_ref[:, pl.ds(pl.multiple_of(j * block, block), block)]
    allowed = (t >= u) & (t <= ends)
    return score, allowed, jnp.where(allowed, 1.0 + score + 0.5 * score * score, 0.0)

def forward_kernel(
    first_ref,
    twin_at_ref,
    own_at_ref,
    is_own_ref,
    twin_ref,
    own_ref,
    weight_ref,
    ends_ref,
    qkv_ref,
    mixed_ref,
    ratio_ref,
    denom_ref,
    key_ref,
    numer_ref,
    sum_ref,
):
    i = pl.program_id(0)
    block = own_ref.shape[0]
    here = pl.ds(pl.multiple_of(i * block, block), block)

    def project(rows_ref):
        qkv_ref[here] = dot_nt(rows_ref[...], weight_ref[...]).astype(jnp.bfloat16)

    pl.when(is_own_ref[i] == 1)(lambda: project(own_ref))
    pl.when(is_own_ref[i] == 0)(lambda: project(twin_ref))
    key_ref[here] = qkv_ref[here, VALUES + FEATS :]
    query = qkv_ref[here, VALUES : VALUES + FEATS]
    own = [head_lanes(query, head) for head in range(2)]
    numer_ref[...] = jnp.zeros_like(numer_ref)
    sum_ref[...] = jnp.zeros_like(sum_ref)

    def step(j, carry):
        there = pl.ds(pl.multiple_of(j * block, block), block)
        for head in range(2):
            columns = pl.ds(head * HEAD_V, HEAD_V)
            _, _, kernel = scores(own[head], key_ref[there], ends_ref, i, j, block)
            folded = kernel[:, :128]
            for c in range(1, block // 128):
                folded = folded + kernel[:, c * 128 : (c + 1) * 128]
            sum_ref[:, pl.ds(head * 128, 128)] += folded
            numer_ref[:, columns] += dot_nn(kernel.astype(jnp.bfloat16), qkv_ref[there, columns])
        return carry

    lax.fori_loop(first_ref[i], i + 1, step, 0)
    for head in range(2):
        columns = pl.ds(head * HEAD_V, HEAD_V)
        denom = jnp.sum(sum_ref[:, pl.ds(head * 128, 128)], axis=1, keepdims=True)
        ratio = numer_ref[:, columns] / denom
        mixed_ref[:, columns] = ratio.astype(jnp.bfloat16)
        ratio_ref[:, columns] = ratio
        denom_ref[:, columns] = jnp.broadcast_to(denom, ratio.shape)

def attention_rows(first, places, ends, twin, own, weight):
    half_rows, model = own.shape
    group_rows = 2 * half_rows
    block = group_rows // 8
    width = VALUES + 2 * FEATS

    def by_rows(columns):
        return pl.BlockSpec((block, columns), lambda i, *_: (i, 0))

    def whole(shape):
        return pl.BlockSpec(shape, lambda i, *_: (0, 0))

    return pl.pallas_call(
        forward_kernel,
        out_shape=[
            jax.ShapeDtypeStruct((group_rows, width), jnp.bfloat16),
            jax.ShapeDtypeStruct((group_rows, VALUES), jnp.bfloat16),
            jax.ShapeDtypeStruct((group_rows, VALUES), jnp.float32),
            jax.ShapeDtypeStruct((group_rows, VALUES), jnp.float32),
        ],
        grid_spec=pltpu.PrefetchScalarGridSpec(
            num_scalar_prefetch=4,
            grid=(8,),
            in_specs=[
                pl.BlockSpec((block, model), lambda i, f, twin_at, own_at, s: (twin_at[i], 0)),
                pl.BlockSpec((block, model), lambda i, f, twin_at, own_at, s: (own_at[i], 0)),
                whole((width, model)),
                whole((1, group_rows)),
            ],
            out_specs=[
                whole((group_rows, width)),
                by_rows(VALUES),
                by_rows(VALUES),
                by_rows(VALUES),
            ],
            scratch_shapes=[
                pltpu.VMEM((group_rows, FEATS), jnp.bfloat16),
                pltpu.VMEM((block, VALUES), jnp.float32),
                pltpu.VMEM((block, 256), jnp.float32),
            ],
        ),
        compiler_params=pltpu.CompilerParams(vmem_limit_bytes=32 << 20),
        cost_estimate=NO_COST,
        name="attention_rows",
    )(first, *places, twin, own, weight, ends)


def backward_kernel(
    first_ref,
    place_ref,
    attn_ref,
    weight_ref,
    qkv_ref,
    ratio_ref,
    denom_ref,
    ends_ref,
    grad_ref,
    key_ref,
    key_sum,
    value_sum,
    query_sum,
):
    i = pl.program_id(0)
    block = attn_ref.shape[0]
    here = pl.ds(pl.multiple_of(i * block, block), block)
    @pl.when(i == 0)
    def _():
        key_ref[...] = qkv_ref[:, VALUES + FEATS:]
        key_sum[...] = jnp.zeros_like(key_sum)
        value_sum[...] = jnp.zeros_like(value_sum)
    mixed_grad = dot_nt(attn_ref[...], weight_ref[...]).astype(jnp.bfloat16).astype(jnp.float32)
    query = qkv_ref[here, VALUES : VALUES + FEATS]
    own = [head_lanes(query, head) for head in range(2)]
    numer_grads, denom_grads = [], []
    for head in range(2):
        columns = pl.ds(head * HEAD_V, HEAD_V)
        grad = mixed_grad[:, head * HEAD_V : (head + 1) * HEAD_V]
        denom = denom_ref[:, columns]
        numer_grads.append((grad / denom).astype(jnp.bfloat16))
        denom_grads.append(-jnp.sum(grad * ratio_ref[:, columns], axis=1, keepdims=True) / denom[:, :1])
    query_sum[...] = jnp.zeros_like(query_sum)

    def step(j, carry):
        there = pl.ds(pl.multiple_of(j * block, block), block)
        keys = key_ref[there]
        key_grads = None
        for head in range(2):
            columns = pl.ds(head * HEAD_V, HEAD_V)
            score, allowed, kernel = scores(own[head], keys, ends_ref, i, j, block)
            kernel_grad = dot_nt(numer_grads[head], qkv_ref[there, columns]) + denom_grads[head]
            score_grad = jnp.where(allowed, kernel_grad * (1.0 + score), 0.0).astype(jnp.bfloat16)
            query_sum[:, pl.ds(head * 128, FEATS)] += dot_nn(score_grad, keys)
            key_grad = dot_tn(score_grad, own[head])
            key_grads = key_grad if key_grads is None else key_grads + key_grad
            value_sum[there, columns] += dot_tn(kernel.astype(jnp.bfloat16), numer_grads[head])
        key_sum[there] += key_grads
        return carry

    lax.fori_loop(first_ref[i], i + 1, step, 0)
    totals = [query_sum[:, pl.ds(head * 128, FEATS)] for head in range(2)]
    query_grad = (head_lanes(totals[0], 0) + head_lanes(totals[1], 1)) * 0.25
    placed = pl.ds(pl.multiple_of(place_ref[i] * block, block), block)
    grad_ref[placed, VALUES : VALUES + FEATS] = query_grad.astype(jnp.bfloat16)

    @pl.when(i == pl.num_programs(0) - 1)
    def _():
        def store(j, carry):
            there = pl.ds(pl.multiple_of(j * block, block), block)
            placed = pl.ds(pl.multiple_of(place_ref[j] * block, block), block)
            grad_ref[placed, :VALUES] = value_sum[there].astype(jnp.bfloat16)
            grad_ref[placed, VALUES + FEATS :] = (key_sum[there] * 0.25).astype(jnp.bfloat16)
            return carry

        lax.fori_loop(0, pl.num_programs(0), store, 0)

def attention_back(first, place, ends, attn_rows, weight, qkv, ratio, denom):
    group_rows, model = attn_rows.shape
    block = group_rows // 8
    width = VALUES + 2 * FEATS

    def by_rows(columns):
        return pl.BlockSpec((block, columns), lambda i, *_: (i, 0))

    def whole(shape):
        return pl.BlockSpec(shape, lambda i, *_: (0, 0))

    return pl.pallas_call(
        backward_kernel,
        out_shape=jax.ShapeDtypeStruct((group_rows, width), jnp.bfloat16),
        grid_spec=pltpu.PrefetchScalarGridSpec(
            num_scalar_prefetch=2,
            grid=(8,),
            in_specs=[
                by_rows(model),
                whole((VALUES, model)),
                whole((group_rows, width)),
                by_rows(VALUES),
                by_rows(VALUES),
                whole((1, group_rows)),
            ],
            out_specs=whole((group_rows, width)),
            scratch_shapes=[
                pltpu.VMEM((group_rows, FEATS), jnp.bfloat16),
                pltpu.VMEM((group_rows, FEATS), jnp.float32),
                pltpu.VMEM((group_rows, VALUES), jnp.float32),
                pltpu.VMEM((block, 256), jnp.float32),
            ],
        ),
        compiler_params=pltpu.CompilerParams(vmem_limit_bytes=40 << 20),
        cost_estimate=NO_COST,
        name="attention_back",
    )(first, place, attn_rows, weight, qkv, ratio, denom, ends)


def bounds(doc_row):
    group_rows = doc_row.shape[0]; block = group_rows // 8
    ends = jnp.sum(doc_row[:, None] <= doc_row[None, :], axis=0, dtype=jnp.int32) - 1
    starts = block * jnp.arange(8, dtype=jnp.int32)
    first = jnp.sum(ends[block - 1 :: block][None, :] < starts[:, None], axis=1, dtype=jnp.int32)
    return first, ends.reshape(1, group_rows)


def ffn_kernel(pieces, order_ref, rows_ref, grad_ref, *refs):
    weights = refs[:4]
    act_grad_ref, hidden_ref, part_ref, held, sems = refs[-5:]

    @pl.when(pl.program_id(0) == 0)
    def _():
        copies = [
            pltpu.make_async_copy(ref, held.at[pl.ds(i * pieces, pieces)], sems.at[i])
            for i, ref in enumerate(weights)
        ]
        for copy in copies:
            copy.start()
        for copy in copies:
            copy.wait()

    rows = rows_ref[...]
    for half in range(2):
        at = 2 * half * pieces
        gate = dot_nt(held[pl.ds(at, pieces)], rows)
        up = dot_nt(held[pl.ds(at + pieces, pieces)], rows)
        grad = grad_ref[pl.ds(half * pieces, pieces)]
        sigmoid = jax.nn.sigmoid(gate)
        act = gate * sigmoid
        hidden_ref[pl.ds(half * pieces, pieces)] = (act * up).astype(jnp.bfloat16)
        act_grad_ref[pl.ds(at, pieces)] = (
            grad * up * (sigmoid * (1.0 + gate * (1.0 - sigmoid)))
        ).astype(jnp.bfloat16)
        act_grad_ref[pl.ds(at + pieces, pieces)] = (grad * act).astype(jnp.bfloat16)
    part_ref[...] = dot_tn(act_grad_ref[...], held[...]).astype(jnp.bfloat16)


def ffn_rows(order, rows, grad_hidden, weights, earlier=()):
    group_rows, model = rows.shape
    pieces = weights[0].shape[0]
    block = group_rows // 8
    blocks = order.shape[0]
    anywhere = pl.BlockSpec(memory_space=pl.ANY)
    return pl.pallas_call(
        functools.partial(ffn_kernel, pieces),
        out_shape=[
            jax.ShapeDtypeStruct((4 * pieces, group_rows), jnp.bfloat16),
            jax.ShapeDtypeStruct((2 * pieces, group_rows), jnp.bfloat16),
            jax.ShapeDtypeStruct((blocks * block, model), jnp.bfloat16),
        ],
        grid_spec=pltpu.PrefetchScalarGridSpec(
            num_scalar_prefetch=1,
            grid=(blocks,),
            in_specs=[
                pl.BlockSpec((block, model), lambda i, o: (o[i], 0)),
                pl.BlockSpec((2 * pieces, block), lambda i, o: (0, o[i])),
                *[anywhere] * (4 + len(earlier)),
            ],
            out_specs=[
                pl.BlockSpec((4 * pieces, block), lambda i, o: (0, o[i])),
                pl.BlockSpec((2 * pieces, block), lambda i, o: (0, o[i])),
                pl.BlockSpec((block, model), lambda i, o: (i, 0)),
            ],
            scratch_shapes=[
                pltpu.VMEM((4 * pieces, model), jnp.bfloat16),
                pltpu.SemaphoreType.DMA((4,)),
            ],
        ),
        input_output_aliases={7 + i: i for i in range(len(earlier))},
        compiler_params=pltpu.CompilerParams(vmem_limit_bytes=44 << 20),
        cost_estimate=NO_COST,
        name="ffn_rows",
    )(order, rows, grad_hidden, *weights, *earlier)


def product_kernel(turned, order_ref, rows_ref, weight_ref, part_ref):
    product = dot_tn if turned else dot_nn
    part_ref[...] = product(rows_ref[...], weight_ref[...]).astype(jnp.bfloat16)


def product_rows(order, rows, weight, turned=False):
    group_rows = rows.shape[1 if turned else 0]
    depth, model = weight.shape
    block = group_rows // 8
    blocks = order.shape[0]
    if turned:
        rows_spec = pl.BlockSpec((depth, block), lambda i, o: (0, o[i]))
    else:
        rows_spec = pl.BlockSpec((block, depth), lambda i, o: (o[i], 0))
    return pl.pallas_call(
        functools.partial(product_kernel, turned),
        out_shape=jax.ShapeDtypeStruct((blocks * block, model), jnp.bfloat16),
        grid_spec=pltpu.PrefetchScalarGridSpec(
            num_scalar_prefetch=1,
            grid=(blocks,),
            in_specs=[rows_spec, pl.BlockSpec((depth, model), lambda i, o: (0, 0))],
            out_specs=pl.BlockSpec((block, model), lambda i, o: (i, 0)),
        ),
        compiler_params=pltpu.CompilerParams(vmem_limit_bytes=24 << 20),
        cost_estimate=NO_COST,
        name="product_rows",
    )(order, rows, weight)


def sync(*values):
    return lax.optimization_barrier(values)


def after(value, *others):
    return lax.optimization_barrier((value, *others))[0]


def make_body(y_size):
    y_pairs = [(i, i ^ 1) for i in range(y_size)]
    owner_y_pairs = [(i * 4 + kh, (i ^ 1) * 4 + kh) for i in range(y_size) for kh in (0, 3)]

    def trade(values):
        return lax.ppermute(values, ("k", "h"), [(0, 0), (1, 2), (2, 1), (3, 3)])

    def over_y(values):
        return lax.ppermute(values, "y", y_pairs)

    def over_h(values):
        return lax.ppermute(values, ("k", "h"), [(1, 0), (2, 3)])

    def over_owners(values):
        return lax.ppermute(values, ("y", "k", "h"), owner_y_pairs)

    def from_owner(values):
        twin = lax.ppermute(values, ("k", "h"), [(0, 2), (3, 1)])
        return jnp.where(lax.axis_index("k") == lax.axis_index("h"), values, twin)

    def all_y(total):
        step = 2
        while step < y_size:
            total = total + lax.ppermute(total, "y", [(i, i ^ step) for i in range(y_size)])
            step *= 2
        return total

    def my_half(own, axis=0):
        half = own.shape[axis] // 2
        return lax.dynamic_slice_in_dim(own, (lax.axis_index("y") % 2) * half, half, axis)

    def orders():
        k, l, x = (lax.axis_index(name) for name in SQUARE)
        chips = jnp.array([3, 1, 2, 0], jnp.int32) ^ (2 * l + x)
        return (chips + 4 * (1 - k), chips + 4 * k)

    def places():
        k, l, x = (lax.axis_index(name) for name in SQUARE)
        index = jnp.arange(8, dtype=jnp.int32)

        def slot(block):
            chip = (block % 4) ^ (2 * l + x)
            return jnp.where((chip == 0) | (chip == 3), 3 - chip, chip)

        first_twin = 4 * (1 - k)
        twin_at = slot(jnp.clip(index, first_twin, first_twin + 3))
        own_at = slot(jnp.clip(index, 4 * k, 4 * k + 3))
        is_own = (index // 4 == k).astype(jnp.int32)
        return (twin_at, own_at, is_own), slot(index) + 4 * is_own

    def low(*values):
        return jnp.concatenate(values, axis=0).astype(jnp.bfloat16)

    def scatter_first(mine, from_twin):
        rows = mine.shape[0] // 4
        half = rows // 2

        def chip(start, stop):
            return mine[start:stop].astype(jnp.float32) + from_twin[start:stop]

        first_x = low(chip(0, half), chip(rows, rows + half))
        first_l = low(chip(half, rows), chip(2 * rows + half, 3 * rows))
        rest = (
            chip(rows + half, 2 * rows),
            chip(2 * rows, 2 * rows + half),
            chip(3 * rows, 4 * rows),
        )
        return sync(first_x, first_l), rest

    def scatter_last(got_x, got_l, rest):
        half = got_x.shape[0] // 2
        return sync(low(rest[0] + got_l[:half]), low(rest[1] + got_x[:half]))

    def scatter_end(got_x, got_l, last_x, last_l, rest):
        half = got_x.shape[0] // 2
        own_top = rest[2][:half] + got_x[half:] + last_l
        own_bottom = rest[2][half:] + last_x + got_l[half:]
        return jnp.concatenate([own_top, own_bottom], axis=0)

    def flip(values, name):
        return lax.ppermute(values, name, FLIP)

    def in_order(mine, theirs, axis=0):
        first = lax.axis_index("y") % 2 == 0
        return jnp.where(
            first,
            jnp.concatenate([mine, theirs], axis=axis),
            jnp.concatenate([theirs, mine], axis=axis),
        ).astype(jnp.float32)

    def gather(rows):
        return lax.all_gather(rows, SQUARE, axis=0, tiled=True)

    def low_dot(left, right):
        return dot_nn(left, right).astype(jnp.bfloat16)

    def body(
        tokens,
        gain_one,
        w_query,
        w_key,
        w_value,
        w_out,
        gain_two,
        w_gate,
        w_up,
        w_down,
        doc_ids,
        cotangent,
    ):
        for_twin, for_own = orders()
        halves_at, place = places()
        stacked = jnp.arange(4, dtype=jnp.int32)
        qkv_size = HEAD_V + 2 * FEAT
        head_size = qkv_size + HEAD_V
        head_half = jnp.concatenate(
            [
                my_half(w_value, 1).T,
                my_half(w_query.T),
                my_half(w_key.T),
                my_half(w_out),
                jnp.broadcast_to(doc_ids.astype(jnp.bfloat16), (16, doc_ids.shape[1])),
            ],
            axis=0,
        )
        down_half, gate_half, up_half = my_half(w_down), my_half(w_gate.T), my_half(w_up.T)
        own_tokens = trade(tokens)
        own_tokens = after(own_tokens, head_half, down_half, gate_half, up_half)
        inputs = own_tokens.astype(jnp.float32)
        normed_one, scale_one, low_one = norm_rows(inputs, gain_one)

        head_mine = trade(after(head_half, low_one))
        from_x, from_l, head_mine = sync(flip(low_one, "x"), flip(low_one, "l"), head_mine)
        half = low_one.shape[0] // 2
        qkv_other = over_y(head_mine[:qkv_size])
        own_grad = trade(after(cotangent, head_mine))
        d_top = flip(from_l[:half], "x")
        d_bottom = flip(from_x[half:], "l")
        stack_own = jnp.concatenate([d_top, d_bottom, from_x, from_l, low_one], axis=0)
        stack_own, qkv_other = sync(stack_own, qkv_other)
        stack_twin = flip(stack_own, "k")
        wo_other = over_y(after(head_mine[qkv_size:head_size], qkv_other))
        first, ends = bounds(head_mine[head_size].astype(jnp.int32))
        w_qkv = jnp.concatenate(
            [
                head_mine[:HEAD_V],
                qkv_other[:HEAD_V],
                head_mine[HEAD_V : HEAD_V + FEAT],
                qkv_other[HEAD_V : HEAD_V + FEAT],
                head_mine[HEAD_V + FEAT : qkv_size],
                qkv_other[HEAD_V + FEAT : qkv_size],
            ],
            axis=0,
        )
        stack_twin, w_qkv, own_grad, first = sync(stack_twin, w_qkv, own_grad, first)

        grad_rows = gather(own_grad)
        down_mine = trade(after(down_half, own_grad))
        qkv, mixed_heads, ratio, denom = attention_rows(
            first, halves_at, ends, stack_twin, stack_own, w_qkv
        )
        wo = jnp.concatenate([head_mine[qkv_size:head_size], wo_other], axis=0)
        mixed_heads, down_mine, wo = sync(mixed_heads, down_mine, wo)

        from_twin = flip(product_rows(for_twin, mixed_heads, wo), "k")
        down_other = over_y(down_mine)
        gate_mine = trade(after(gate_half, down_mine))
        (first_x, first_l), rest = scatter_first(
            product_rows(for_own, mixed_heads, wo), from_twin
        )
        got_x, got_l, down_other, gate_mine = sync(
            flip(first_x, "x"), flip(first_l, "l"), down_other, gate_mine
        )
        to_x, to_l = scatter_last(got_x, got_l, rest)
        up_mine = trade(after(up_half, gate_mine))
        gate_other = over_y(gate_mine)
        attn_out = scatter_end(got_x, got_l, flip(to_x, "x"), flip(to_l, "l"), rest)

        residual = inputs + attn_out
        normed_two, scale_two, low_two = norm_rows(residual, gain_two)
        gathered_two = gather(low_two)
        wd = jnp.concatenate([down_mine, down_other], axis=0)
        grad_hidden = dot_nt(wd, after(grad_rows, up_mine, low_two))
        up_other = over_y(up_mine)
        gathered_two, up_other, gate_other, grad_hidden = sync(
            gathered_two, up_other, gate_other, grad_hidden
        )

        weights = (gate_mine, up_mine, gate_other, up_other)
        *acts, parts_twin = ffn_rows(for_twin, gathered_two, grad_hidden, weights)
        from_twin = flip(parts_twin, "k")
        act_grad, hidden, parts_own = ffn_rows(
            for_own, gathered_two, grad_hidden, weights, tuple(acts)
        )
        units = hidden.shape[0] // 2
        unit_acts = {
            "gate": (act_grad[:units], act_grad[2 * units : 3 * units]),
            "up": (act_grad[units : 2 * units], act_grad[3 * units :]),
            "down": (hidden[:units], hidden[units:]),
        }
        unit_rows = {"gate": gathered_two, "up": gathered_two, "down": grad_rows}

        def other_part(name, *deps):
            return low_dot(after(unit_acts[name][1], *deps), unit_rows[name])

        def y_total(name, arrived):
            return all_y((dot_nn(unit_acts[name][0], unit_rows[name]) + arrived).astype(jnp.bfloat16))

        (first_x, first_l), rest = scatter_first(parts_own, from_twin)
        down_part = other_part("down", first_x)
        down_y = over_y(down_part)
        gate_part = other_part("gate", down_part)
        up_part = other_part("up", gate_part)
        got_x, got_l, gate_part, up_part = sync(
            flip(first_x, "x"), flip(first_l, "l"), gate_part, up_part
        )
        to_x, to_l = scatter_last(got_x, got_l, rest)
        late_hidden = after(hidden, to_x)
        ffn_twin = product_rows(for_twin, late_hidden, wd, turned=True)
        ffn_own = product_rows(for_own, late_hidden, wd, turned=True)
        grad_normed_two = scatter_end(got_x, got_l, flip(to_x, "x"), flip(to_l, "l"), rest)
        grad_normed_two, down_y, ffn_twin, ffn_own = sync(
            grad_normed_two, down_y, ffn_twin, ffn_own
        )

        gate_y = over_y(gate_part)
        up_y = over_y(up_part)
        gain_two_part = jnp.sum(grad_normed_two * normed_two, axis=0)
        grad_resid = own_grad.astype(jnp.float32) + norm_back(
            grad_normed_two, normed_two, scale_two, gain_two
        )
        low_resid = grad_resid.astype(jnp.bfloat16)
        grad_attn_rows = gather(low_resid)
        down_total = y_total("down", after(down_y, low_resid))
        down_h = over_h(down_total)
        ffn_from_twin = flip(after(ffn_twin, low_resid), "k")
        (first_x, first_l), rest = scatter_first(ffn_own, ffn_from_twin)
        grad_attn_rows, gate_y, down_h, first_x, first_l = sync(
            grad_attn_rows, gate_y, down_h, first_x, first_l
        )

        gate_total = y_total("gate", gate_y)
        gate_h = over_h(gate_total)
        down_total = down_total + down_h
        down_back = over_owners(down_total)
        grad_qkv = attention_back(
            first, place, ends, after(grad_attn_rows, gate_total), wo, qkv, ratio, denom
        )
        grad_qkv, got_x, got_l, up_y, gate_h, down_back = sync(
            grad_qkv, flip(first_x, "x"), flip(first_l, "l"), up_y, gate_h, down_back
        )

        half_rows = stack_own.shape[0]
        to_x, to_l = scatter_last(got_x, got_l, rest)
        from_twin = flip(product_rows(stacked, grad_qkv, w_qkv), "k")
        one_own = product_rows(stacked + 4, grad_qkv, w_qkv)
        ffn_out = scatter_end(got_x, got_l, flip(to_x, "x"), flip(to_l, "l"), rest)
        (first_x, first_l), rest = scatter_first(one_own, from_twin)
        up_total = y_total("up", after(up_y, first_x))
        up_h = over_h(up_total)
        late_qkv = after(grad_qkv, up_total)
        qkv_part = dot_tn(late_qkv[:half_rows], stack_twin) + dot_tn(
            late_qkv[half_rows:], stack_own
        )
        out_part = dot_tn(after(mixed_heads, up_total), grad_attn_rows)

        def one_head(which):
            at_query = VALUES + which * FEAT
            return jnp.concatenate(
                [
                    qkv_part[which * HEAD_V : (which + 1) * HEAD_V],
                    qkv_part[at_query : at_query + FEAT],
                    qkv_part[at_query + FEATS : at_query + FEATS + FEAT],
                    out_part[which * HEAD_V : (which + 1) * HEAD_V],
                ],
                axis=0,
            )

        head_y = over_y(one_head(1).astype(jnp.bfloat16))
        block_out = trade((residual + ffn_out).astype(jnp.bfloat16))
        got_x, got_l, block_out = sync(flip(first_x, "x"), flip(first_l, "l"), block_out)
        to_x, to_l = scatter_last(got_x, got_l, rest)
        gate_total = gate_total + gate_h
        gate_back = over_owners(gate_total)
        grad_normed_one = scatter_end(got_x, got_l, flip(to_x, "x"), flip(to_l, "l"), rest)
        grad_normed_one, head_y, gate_back = sync(grad_normed_one, head_y, gate_back)

        grad_tokens = grad_resid + norm_back(grad_normed_one, normed_one, scale_one, gain_one)
        low_tokens = grad_tokens.astype(jnp.bfloat16)
        grad_tokens = trade(low_tokens).astype(jnp.float32)
        head_total = all_y((one_head(0) + head_y).astype(jnp.bfloat16))
        head_h = over_h(head_total)
        gain_one_part = jnp.sum(after(qkv_part, low_tokens) * w_qkv, axis=0) / gain_one
        gain_grads = jnp.stack([gain_one_part, gain_two_part])
        for name in ("k", "x", "l", "h"):
            gain_grads = gain_grads + flip(gain_grads, name)
        step = 1
        while step < y_size:
            gain_grads = gain_grads + lax.ppermute(
                gain_grads, "y", [(i, i ^ step) for i in range(y_size)]
            )
            step *= 2
        up_total = up_total + up_h
        up_back = over_owners(up_total)
        down_total, down_back = from_owner(down_total), from_owner(down_back)
        gate_total, gate_back = from_owner(gate_total), from_owner(gate_back)
        up_total = from_owner(up_total)
        head_total = head_total + head_h
        head_back = over_owners(head_total)
        head_total = from_owner(head_total)
        up_back = from_owner(up_back)
        head_back = from_owner(head_back)

        def head_grad(start, stop):
            return in_order(head_total[start:stop], head_back[start:stop])

        return (
            block_out,
            grad_tokens,
            gain_grads[0],
            head_grad(HEAD_V, HEAD_V + FEAT).T,
            head_grad(HEAD_V + FEAT, qkv_size).T,
            in_order(head_total[:HEAD_V].T, head_back[:HEAD_V].T, 1),
            head_grad(qkv_size, head_size),
            gain_grads[1],
            in_order(gate_total, gate_back).T,
            in_order(up_total, up_back).T,
            in_order(down_total, down_back),
        )

    return body


def solution(mesh):
    dp_size, tensor_size = mesh.devices.shape
    fine = Mesh(mesh.devices.reshape(dp_size // 2, 2, 2, 2, tensor_size // 4), ALL_AXES)
    rows = P(ALL_AXES, None)
    shard = ("h", "l", "x")
    in_specs = (
        rows,
        P(),
        P(None, shard),
        P(None, shard),
        P(None, shard),
        P(shard, None),
        P(),
        P(None, shard),
        P(None, shard),
        P(shard, None),
        P(("y", "k"), None),
        rows,
    )
    out_specs = (
        rows,
        rows,
        P(),
        P(None, shard),
        P(None, shard),
        P(None, shard),
        P(shard, None),
        P(),
        P(None, shard),
        P(None, shard),
        P(shard, None),
    )
    return jax.shard_map(
        make_body(dp_size // 2), mesh=fine, in_specs=in_specs, out_specs=out_specs, check_vma=False
    )
```

```python
import functools

import jax
import jax.numpy as jnp
from jax import lax
from jax.experimental import pallas as pl
from jax.experimental.pallas import tpu as pltpu
from jax.sharding import Mesh
from jax.sharding import PartitionSpec as P

FEAT = 16
HEAD_V = 128
EPS = 1e-05
VALUES = 2 * HEAD_V
FEATS = 2 * FEAT
NO_COST = pl.CostEstimate(flops=1, bytes_accessed=1, transcendentals=0)

ALL_AXES = ("y", "k", "h", "l", "x")
FLIP = [(0, 1), (1, 0)]
SQUARE = ("k", "l", "x")


def norm_rows(values, gain_vec):
    row_scale = lax.rsqrt(jnp.mean(values * values, axis=-1, keepdims=True) + EPS)
    normed = values * row_scale
    return (normed, row_scale, (normed * gain_vec).astype(jnp.bfloat16))


def norm_back(grad_normed, normed, row_scale, gain_vec):
    weighted = grad_normed * gain_vec
    inner_mean = jnp.mean(weighted * normed, axis=-1, keepdims=True)
    return row_scale * (weighted - normed * inner_mean)


def dot_nn(left_mat, right_mat):
    return jnp.dot(left_mat, right_mat, preferred_element_type=jnp.float32)


def dot_tn(left_mat, right_mat):
    return lax.dot_general(
        left_mat, right_mat, (((0,), (0,)), ((), ())), preferred_element_type=jnp.float32
    )


def dot_nt(left_mat, right_mat):
    return lax.dot_general(
        left_mat, right_mat, (((1,), (1,)), ((), ())), preferred_element_type=jnp.float32
    )


def head_lanes(values, head):
    lane = lax.broadcasted_iota(jnp.int32, values.shape, 1)
    return jnp.where((lane >= head * FEAT) & (lane < (head + 1) * FEAT), values, jnp.zeros_like(values))

def scores(query, keys, ends_ref, i, j, block):
    score = dot_nt(query, keys) * 0.25
    t = i * block + lax.broadcasted_iota(jnp.int32, score.shape, 0)
    u = j * block + lax.broadcasted_iota(jnp.int32, score.shape, 1)
    ends = ends_ref[:, pl.ds(pl.multiple_of(j * block, block), block)]
    allowed = (t >= u) & (t <= ends)
    return score, allowed, jnp.where(allowed, 1.0 + score + 0.5 * score * score, 0.0)

def forward_kernel(
    first_ref,
    twin_at_ref,
    own_at_ref,
    is_own_ref,
    twin_ref,
    own_ref,
    weight_ref,
    ends_ref,
    qkv_ref,
    mixed_ref,
    ratio_ref,
    denom_ref,
    key_ref,
    numer_ref,
    sum_ref,
):
    i = pl.program_id(0)
    block = own_ref.shape[0]
    here = pl.ds(pl.multiple_of(i * block, block), block)

    def project(rows_ref):
        qkv_ref[here] = dot_nt(rows_ref[...], weight_ref[...]).astype(jnp.bfloat16)

    pl.when(is_own_ref[i] == 1)(lambda: project(own_ref))
    pl.when(is_own_ref[i] == 0)(lambda: project(twin_ref))
    key_ref[here] = qkv_ref[here, VALUES + FEATS :]
    query = qkv_ref[here, VALUES : VALUES + FEATS]
    own = [head_lanes(query, head) for head in range(2)]
    numer_ref[...] = jnp.zeros_like(numer_ref)
    sum_ref[...] = jnp.zeros_like(sum_ref)

    def step(j, carry):
        there = pl.ds(pl.multiple_of(j * block, block), block)
        for head in range(2):
            columns = pl.ds(head * HEAD_V, HEAD_V)
            _, _, kernel = scores(own[head], key_ref[there], ends_ref, i, j, block)
            folded = kernel[:, :128]
            for c in range(1, block // 128):
                folded = folded + kernel[:, c * 128 : (c + 1) * 128]
            sum_ref[:, pl.ds(head * 128, 128)] += folded
            numer_ref[:, columns] += dot_nn(kernel.astype(jnp.bfloat16), qkv_ref[there, columns])
        return carry

    lax.fori_loop(first_ref[i], i + 1, step, 0)
    for head in range(2):
        columns = pl.ds(head * HEAD_V, HEAD_V)
        denom = jnp.sum(sum_ref[:, pl.ds(head * 128, 128)], axis=1, keepdims=True)
        ratio = numer_ref[:, columns] / denom
        mixed_ref[:, columns] = ratio.astype(jnp.bfloat16)
        ratio_ref[:, columns] = ratio
        denom_ref[:, columns] = jnp.broadcast_to(denom, ratio.shape)

def attention_rows(first, places, ends, twin, own, weight):
    half_rows, model = own.shape
    group_rows = 2 * half_rows
    block = group_rows // 8
    width = VALUES + 2 * FEATS

    def by_rows(columns):
        return pl.BlockSpec((block, columns), lambda i, *_: (i, 0))

    def whole(shape):
        return pl.BlockSpec(shape, lambda i, *_: (0, 0))

    return pl.pallas_call(
        forward_kernel,
        out_shape=[
            jax.ShapeDtypeStruct((group_rows, width), jnp.bfloat16),
            jax.ShapeDtypeStruct((group_rows, VALUES), jnp.bfloat16),
            jax.ShapeDtypeStruct((group_rows, VALUES), jnp.float32),
            jax.ShapeDtypeStruct((group_rows, VALUES), jnp.float32),
        ],
        grid_spec=pltpu.PrefetchScalarGridSpec(
            num_scalar_prefetch=4,
            grid=(8,),
            in_specs=[
                pl.BlockSpec((block, model), lambda i, f, twin_at, own_at, s: (twin_at[i], 0)),
                pl.BlockSpec((block, model), lambda i, f, twin_at, own_at, s: (own_at[i], 0)),
                whole((width, model)),
                whole((1, group_rows)),
            ],
            out_specs=[
                whole((group_rows, width)),
                by_rows(VALUES),
                by_rows(VALUES),
                by_rows(VALUES),
            ],
            scratch_shapes=[
                pltpu.VMEM((group_rows, FEATS), jnp.bfloat16),
                pltpu.VMEM((block, VALUES), jnp.float32),
                pltpu.VMEM((block, 256), jnp.float32),
            ],
        ),
        compiler_params=pltpu.CompilerParams(vmem_limit_bytes=32 << 20),
        cost_estimate=NO_COST,
        name="attention_rows",
    )(first, *places, twin, own, weight, ends)


def backward_kernel(
    first_ref,
    place_ref,
    attn_ref,
    weight_ref,
    qkv_ref,
    ratio_ref,
    denom_ref,
    ends_ref,
    grad_ref,
    key_ref,
    key_sum,
    value_sum,
    query_sum,
):
    i = pl.program_id(0)
    block = attn_ref.shape[0]
    here = pl.ds(pl.multiple_of(i * block, block), block)
    @pl.when(i == 0)
    def _():
        key_ref[...] = qkv_ref[:, VALUES + FEATS:]
        key_sum[...] = jnp.zeros_like(key_sum)
        value_sum[...] = jnp.zeros_like(value_sum)
    mixed_grad = dot_nt(attn_ref[...], weight_ref[...]).astype(jnp.bfloat16).astype(jnp.float32)
    query = qkv_ref[here, VALUES : VALUES + FEATS]
    own = [head_lanes(query, head) for head in range(2)]
    numer_grads, denom_grads = [], []
    for head in range(2):
        columns = pl.ds(head * HEAD_V, HEAD_V)
        grad = mixed_grad[:, head * HEAD_V : (head + 1) * HEAD_V]
        denom = denom_ref[:, columns]
        numer_grads.append((grad / denom).astype(jnp.bfloat16))
        denom_grads.append(-jnp.sum(grad * ratio_ref[:, columns], axis=1, keepdims=True) / denom[:, :1])
    query_sum[...] = jnp.zeros_like(query_sum)

    def step(j, carry):
        there = pl.ds(pl.multiple_of(j * block, block), block)
        keys = key_ref[there]
        key_grads = None
        for head in range(2):
            columns = pl.ds(head * HEAD_V, HEAD_V)
            score, allowed, kernel = scores(own[head], keys, ends_ref, i, j, block)
            kernel_grad = dot_nt(numer_grads[head], qkv_ref[there, columns]) + denom_grads[head]
            score_grad = jnp.where(allowed, kernel_grad * (1.0 + score), 0.0).astype(jnp.bfloat16)
            query_sum[:, pl.ds(head * 128, FEATS)] += dot_nn(score_grad, keys)
            key_grad = dot_tn(score_grad, own[head])
            key_grads = key_grad if key_grads is None else key_grads + key_grad
            value_sum[there, columns] += dot_tn(kernel.astype(jnp.bfloat16), numer_grads[head])
        key_sum[there] += key_grads
        return carry

    lax.fori_loop(first_ref[i], i + 1, step, 0)
    totals = [query_sum[:, pl.ds(head * 128, FEATS)] for head in range(2)]
    query_grad = (head_lanes(totals[0], 0) + head_lanes(totals[1], 1)) * 0.25
    placed = pl.ds(pl.multiple_of(place_ref[i] * block, block), block)
    grad_ref[placed, VALUES : VALUES + FEATS] = query_grad.astype(jnp.bfloat16)

    @pl.when(i == pl.num_programs(0) - 1)
    def _():
        def store(j, carry):
            there = pl.ds(pl.multiple_of(j * block, block), block)
            placed = pl.ds(pl.multiple_of(place_ref[j] * block, block), block)
            grad_ref[placed, :VALUES] = value_sum[there].astype(jnp.bfloat16)
            grad_ref[placed, VALUES + FEATS :] = (key_sum[there] * 0.25).astype(jnp.bfloat16)
            return carry

        lax.fori_loop(0, pl.num_programs(0), store, 0)

def attention_back(first, place, ends, attn_rows, weight, qkv, ratio, denom):
    group_rows, model = attn_rows.shape
    block = group_rows // 8
    width = VALUES + 2 * FEATS

    def by_rows(columns):
        return pl.BlockSpec((block, columns), lambda i, *_: (i, 0))

    def whole(shape):
        return pl.BlockSpec(shape, lambda i, *_: (0, 0))

    return pl.pallas_call(
        backward_kernel,
        out_shape=jax.ShapeDtypeStruct((group_rows, width), jnp.bfloat16),
        grid_spec=pltpu.PrefetchScalarGridSpec(
            num_scalar_prefetch=2,
            grid=(8,),
            in_specs=[
                by_rows(model),
                whole((VALUES, model)),
                whole((group_rows, width)),
                by_rows(VALUES),
                by_rows(VALUES),
                whole((1, group_rows)),
            ],
            out_specs=whole((group_rows, width)),
            scratch_shapes=[
                pltpu.VMEM((group_rows, FEATS), jnp.bfloat16),
                pltpu.VMEM((group_rows, FEATS), jnp.float32),
                pltpu.VMEM((group_rows, VALUES), jnp.float32),
                pltpu.VMEM((block, 256), jnp.float32),
            ],
        ),
        compiler_params=pltpu.CompilerParams(vmem_limit_bytes=40 << 20),
        cost_estimate=NO_COST,
        name="attention_back",
    )(first, place, attn_rows, weight, qkv, ratio, denom, ends)


def bounds(doc_row):
    group_rows = doc_row.shape[0]; block = group_rows // 8
    ends = jnp.sum(doc_row[:, None] <= doc_row[None, :], axis=0, dtype=jnp.int32) - 1
    starts = block * jnp.arange(8, dtype=jnp.int32)
    first = jnp.sum(ends[block - 1 :: block][None, :] < starts[:, None], axis=1, dtype=jnp.int32)
    return first, ends.reshape(1, group_rows)


def ffn_kernel(pieces, order_ref, rows_ref, grad_ref, *refs):
    weights = refs[:4]
    act_grad_ref, hidden_ref, part_ref, held, sems = refs[-5:]

    @pl.when(pl.program_id(0) == 0)
    def _():
        copies = [
            pltpu.make_async_copy(ref, held.at[pl.ds(i * pieces, pieces)], sems.at[i])
            for i, ref in enumerate(weights)
        ]
        for copy in copies:
            copy.start()
        for copy in copies:
            copy.wait()

    rows = rows_ref[...]
    for half in range(2):
        at = 2 * half * pieces
        gate = dot_nt(held[pl.ds(at, pieces)], rows)
        up = dot_nt(held[pl.ds(at + pieces, pieces)], rows)
        grad = grad_ref[pl.ds(half * pieces, pieces)]
        sigmoid = jax.nn.sigmoid(gate)
        act = gate * sigmoid
        hidden_ref[pl.ds(half * pieces, pieces)] = (act * up).astype(jnp.bfloat16)
        act_grad_ref[pl.ds(at, pieces)] = (
            grad * up * (sigmoid * (1.0 + gate * (1.0 - sigmoid)))
        ).astype(jnp.bfloat16)
        act_grad_ref[pl.ds(at + pieces, pieces)] = (grad * act).astype(jnp.bfloat16)
    part_ref[...] = dot_tn(act_grad_ref[...], held[...]).astype(jnp.bfloat16)


def ffn_rows(order, rows, grad_hidden, weights, earlier=()):
    group_rows, model = rows.shape
    pieces = weights[0].shape[0]
    block = group_rows // 8
    blocks = order.shape[0]
    anywhere = pl.BlockSpec(memory_space=pl.ANY)
    return pl.pallas_call(
        functools.partial(ffn_kernel, pieces),
        out_shape=[
            jax.ShapeDtypeStruct((4 * pieces, group_rows), jnp.bfloat16),
            jax.ShapeDtypeStruct((2 * pieces, group_rows), jnp.bfloat16),
            jax.ShapeDtypeStruct((blocks * block, model), jnp.bfloat16),
        ],
        grid_spec=pltpu.PrefetchScalarGridSpec(
            num_scalar_prefetch=1,
            grid=(blocks,),
            in_specs=[
                pl.BlockSpec((block, model), lambda i, o: (o[i], 0)),
                pl.BlockSpec((2 * pieces, block), lambda i, o: (0, o[i])),
                *[anywhere] * (4 + len(earlier)),
            ],
            out_specs=[
                pl.BlockSpec((4 * pieces, block), lambda i, o: (0, o[i])),
                pl.BlockSpec((2 * pieces, block), lambda i, o: (0, o[i])),
                pl.BlockSpec((block, model), lambda i, o: (i, 0)),
            ],
            scratch_shapes=[
                pltpu.VMEM((4 * pieces, model), jnp.bfloat16),
                pltpu.SemaphoreType.DMA((4,)),
            ],
        ),
        input_output_aliases={7 + i: i for i in range(len(earlier))},
        compiler_params=pltpu.CompilerParams(vmem_limit_bytes=44 << 20),
        cost_estimate=NO_COST,
        name="ffn_rows",
    )(order, rows, grad_hidden, *weights, *earlier)


def product_kernel(turned, order_ref, rows_ref, weight_ref, part_ref):
    product = dot_tn if turned else dot_nn
    part_ref[...] = product(rows_ref[...], weight_ref[...]).astype(jnp.bfloat16)


def product_rows(order, rows, weight, turned=False):
    group_rows = rows.shape[1 if turned else 0]
    depth, model = weight.shape
    block = group_rows // 8
    blocks = order.shape[0]
    if turned:
        rows_spec = pl.BlockSpec((depth, block), lambda i, o: (0, o[i]))
    else:
        rows_spec = pl.BlockSpec((block, depth), lambda i, o: (o[i], 0))
    return pl.pallas_call(
        functools.partial(product_kernel, turned),
        out_shape=jax.ShapeDtypeStruct((blocks * block, model), jnp.bfloat16),
        grid_spec=pltpu.PrefetchScalarGridSpec(
            num_scalar_prefetch=1,
            grid=(blocks,),
            in_specs=[rows_spec, pl.BlockSpec((depth, model), lambda i, o: (0, 0))],
            out_specs=pl.BlockSpec((block, model), lambda i, o: (i, 0)),
        ),
        compiler_params=pltpu.CompilerParams(vmem_limit_bytes=24 << 20),
        cost_estimate=NO_COST,
        name="product_rows",
    )(order, rows, weight)


def unit_kernel(with_arrived, acts_ref, rows_ref, *refs):
    total = dot_nn(acts_ref[...], rows_ref[...])
    if with_arrived:
        total = total + refs[0][...]
    refs[-1][...] = total.astype(jnp.bfloat16)


def unit_grad(acts, piece, pieces, rows, arrived=None):
    units = acts.shape[0] // pieces
    group_rows, model = rows.shape
    columns = model // 4
    part = pl.BlockSpec((units, columns), lambda i: (0, i))
    return pl.pallas_call(
        functools.partial(unit_kernel, arrived is not None),
        out_shape=jax.ShapeDtypeStruct((units, model), jnp.bfloat16),
        grid=(4,),
        in_specs=[
            pl.BlockSpec((units, group_rows), lambda i: (piece, 0)),
            pl.BlockSpec((group_rows, columns), lambda i: (0, i)),
            *([] if arrived is None else [part]),
        ],
        out_specs=part,
        compiler_params=pltpu.CompilerParams(vmem_limit_bytes=24 << 20),
        cost_estimate=NO_COST,
        name="unit_grad",
    )(acts, rows, *([] if arrived is None else [arrived]))


def hidden_kernel(mine_ref, other_ref, rows_ref, grad_ref):
    half = mine_ref.shape[0]
    grad_ref[pl.ds(0, half)] = dot_nt(mine_ref[...], rows_ref[...])
    grad_ref[pl.ds(half, half)] = dot_nt(other_ref[...], rows_ref[...])


def hidden_grad(mine, other, rows):
    half, model = mine.shape
    group_rows = rows.shape[0]
    block = group_rows // 4
    weight = pl.BlockSpec((half, model), lambda i: (0, 0))
    return pl.pallas_call(
        hidden_kernel,
        out_shape=jax.ShapeDtypeStruct((2 * half, group_rows), jnp.float32),
        grid=(4,),
        in_specs=[weight, weight, pl.BlockSpec((block, model), lambda i: (i, 0))],
        out_specs=pl.BlockSpec((2 * half, block), lambda i: (0, i)),
        compiler_params=pltpu.CompilerParams(vmem_limit_bytes=28 << 20),
        cost_estimate=NO_COST,
        name="hidden_grad",
    )(mine, other, rows)


def head_kernel(
    qkv_ref, twin_ref, own_ref, mixed_ref, attn_ref, weight_ref, gain_ref, mine_ref, other_ref, sum_ref
):
    half = twin_ref.shape[0]
    qkv = dot_tn(qkv_ref[pl.ds(0, half)], twin_ref[...]) + dot_tn(
        qkv_ref[pl.ds(half, half)], own_ref[...]
    )
    out = dot_tn(mixed_ref[...], attn_ref[...])
    gain_grad = jnp.sum(qkv * weight_ref[...].astype(jnp.float32), axis=0, keepdims=True)
    sum_ref[...] = gain_grad / gain_ref[...]
    for which, ref in enumerate((mine_ref, other_ref)):
        at = VALUES + which * FEAT
        ref[pl.ds(0, HEAD_V)] = qkv[which * HEAD_V : (which + 1) * HEAD_V].astype(ref.dtype)
        ref[pl.ds(HEAD_V, FEAT)] = qkv[at : at + FEAT].astype(ref.dtype)
        ref[pl.ds(HEAD_V + FEAT, FEAT)] = qkv[at + FEATS : at + FEATS + FEAT].astype(ref.dtype)
        ref[pl.ds(HEAD_V + 2 * FEAT, HEAD_V)] = out[which * HEAD_V : (which + 1) * HEAD_V].astype(
            ref.dtype
        )


def head_grads(qkv, twin, own, mixed, attn_rows, weight, gain):
    group_rows, model = attn_rows.shape
    columns = model // 4
    size = 2 * HEAD_V + 2 * FEAT

    def whole(values):
        return pl.BlockSpec(values.shape, lambda i: (0, 0))

    def part(rows):
        return pl.BlockSpec((rows, columns), lambda i: (0, i))

    return pl.pallas_call(
        head_kernel,
        out_shape=[
            jax.ShapeDtypeStruct((size, model), jnp.float32),
            jax.ShapeDtypeStruct((size, model), jnp.bfloat16),
            jax.ShapeDtypeStruct((1, model), jnp.float32),
        ],
        grid=(4,),
        in_specs=[
            whole(qkv),
            part(group_rows // 2),
            part(group_rows // 2),
            whole(mixed),
            part(group_rows),
            part(weight.shape[0]),
            part(1),
        ],
        out_specs=[part(size), part(size), part(1)],
        compiler_params=pltpu.CompilerParams(vmem_limit_bytes=32 << 20),
        cost_estimate=NO_COST,
        name="head_grads",
    )(qkv, twin, own, mixed, attn_rows, weight, gain.reshape(1, model))


def chosen(flags_ref, own_ref, twin_ref):
    return jnp.where(flags_ref[1] == 1, own_ref[...], twin_ref[...]).astype(jnp.float32)


def finish_kernel(flags_ref, mine_ref, mine_twin_ref, theirs_ref, theirs_twin_ref, grad_ref):
    half = mine_ref.shape[0]
    mine, theirs = pl.ds(flags_ref[0] * half, half), pl.ds((1 - flags_ref[0]) * half, half)
    grad_ref[mine] = chosen(flags_ref, mine_ref, mine_twin_ref)
    grad_ref[theirs] = chosen(flags_ref, theirs_ref, theirs_twin_ref)


def finish_unit(flags, *parts):
    half, model = parts[0].shape
    columns = model // 4
    part = pl.BlockSpec((half, columns), lambda i, f: (0, i))
    return pl.pallas_call(
        finish_kernel,
        out_shape=jax.ShapeDtypeStruct((2 * half, model), jnp.float32),
        grid_spec=pltpu.PrefetchScalarGridSpec(
            num_scalar_prefetch=1,
            grid=(4,),
            in_specs=[part] * 4,
            out_specs=pl.BlockSpec((2 * half, columns), lambda i, f: (0, i)),
        ),
        compiler_params=pltpu.CompilerParams(vmem_limit_bytes=24 << 20),
        cost_estimate=NO_COST,
        name="finish_unit",
    )(flags, *parts)


def finish_head_kernel(
    flags_ref, mine_ref, mine_twin_ref, theirs_ref, theirs_twin_ref, query_ref, key_ref, value_ref, out_ref
):
    halves = (
        (flags_ref[0], chosen(flags_ref, mine_ref, mine_twin_ref)),
        (1 - flags_ref[0], chosen(flags_ref, theirs_ref, theirs_twin_ref)),
    )
    for at, grads in halves:
        features = pl.ds(pl.multiple_of(at * FEAT, FEAT), FEAT)
        values = pl.ds(pl.multiple_of(at * HEAD_V, HEAD_V), HEAD_V)
        value_ref[:, values] = grads[:HEAD_V].T
        query_ref[features] = grads[HEAD_V : HEAD_V + FEAT]
        key_ref[features] = grads[HEAD_V + FEAT : HEAD_V + 2 * FEAT]
        out_ref[values] = grads[HEAD_V + 2 * FEAT :]


def finish_head(flags, *parts):
    size, model = parts[0].shape
    columns = model // 4

    def part(rows):
        return pl.BlockSpec((rows, columns), lambda i, f: (0, i))

    return pl.pallas_call(
        finish_head_kernel,
        out_shape=[
            jax.ShapeDtypeStruct((FEATS, model), jnp.float32),
            jax.ShapeDtypeStruct((FEATS, model), jnp.float32),
            jax.ShapeDtypeStruct((model, VALUES), jnp.float32),
            jax.ShapeDtypeStruct((VALUES, model), jnp.float32),
        ],
        grid_spec=pltpu.PrefetchScalarGridSpec(
            num_scalar_prefetch=1,
            grid=(4,),
            in_specs=[part(size)] * 4,
            out_specs=[
                part(FEATS),
                part(FEATS),
                pl.BlockSpec((columns, VALUES), lambda i, f: (i, 0)),
                part(VALUES),
            ],
        ),
        compiler_params=pltpu.CompilerParams(vmem_limit_bytes=24 << 20),
        cost_estimate=NO_COST,
        name="finish_head",
    )(flags, *parts)


def sync(*values):
    return lax.optimization_barrier(values)


def after(value, *others):
    return lax.optimization_barrier((value, *others))[0]


def make_body(y_size):
    y_pairs = [(i, i ^ 1) for i in range(y_size)]
    owner_y_pairs = [(i * 4 + kh, (i ^ 1) * 4 + kh) for i in range(y_size) for kh in (0, 3)]

    cross_pairs = [(i * 4 + kh, (i ^ 1) * 4 + (kh ^ 2)) for i in range(y_size) for kh in (0, 3)]

    def trade(values):
        return lax.ppermute(values, ("k", "h"), [(0, 0), (1, 2), (2, 1), (3, 3)])

    def over_y(values):
        return lax.ppermute(values, "y", y_pairs)

    def over_h(values):
        return lax.ppermute(values, ("k", "h"), [(1, 0), (2, 3)])

    def over_owners(values):
        return lax.ppermute(values, ("y", "k", "h"), owner_y_pairs)

    def to_twin(values):
        return lax.ppermute(values, ("k", "h"), [(0, 2), (3, 1)])

    def across(values):
        return lax.ppermute(values, ("y", "k", "h"), cross_pairs)

    def all_y(total):
        step = 2
        while step < y_size:
            total = total + lax.ppermute(total, "y", [(i, i ^ step) for i in range(y_size)])
            step *= 2
        return total

    def my_half(own, axis=0):
        half = own.shape[axis] // 2
        return lax.dynamic_slice_in_dim(own, (lax.axis_index("y") % 2) * half, half, axis)

    def orders():
        k, l, x = (lax.axis_index(name) for name in SQUARE)
        chips = jnp.array([3, 1, 2, 0], jnp.int32) ^ (2 * l + x)
        return (chips + 4 * (1 - k), chips + 4 * k)

    def places():
        k, l, x = (lax.axis_index(name) for name in SQUARE)
        index = jnp.arange(8, dtype=jnp.int32)

        def slot(block):
            chip = (block % 4) ^ (2 * l + x)
            return jnp.where((chip == 0) | (chip == 3), 3 - chip, chip)

        first_twin = 4 * (1 - k)
        twin_at = slot(jnp.clip(index, first_twin, first_twin + 3))
        own_at = slot(jnp.clip(index, 4 * k, 4 * k + 3))
        is_own = (index // 4 == k).astype(jnp.int32)
        return (twin_at, own_at, is_own), slot(index) + 4 * is_own

    def low(*values):
        return jnp.concatenate(values, axis=0).astype(jnp.bfloat16)

    def scatter_first(mine, from_twin):
        rows = mine.shape[0] // 4
        half = rows // 2

        def chip(start, stop):
            return mine[start:stop].astype(jnp.float32) + from_twin[start:stop]

        first_x = low(chip(0, half), chip(rows, rows + half))
        first_l = low(chip(half, rows), chip(2 * rows + half, 3 * rows))
        rest = (
            chip(rows + half, 2 * rows),
            chip(2 * rows, 2 * rows + half),
            chip(3 * rows, 4 * rows),
        )
        return sync(first_x, first_l), rest

    def scatter_last(got_x, got_l, rest):
        half = got_x.shape[0] // 2
        return sync(low(rest[0] + got_l[:half]), low(rest[1] + got_x[:half]))

    def scatter_end(got_x, got_l, last_x, last_l, rest):
        half = got_x.shape[0] // 2
        own_top = rest[2][:half] + got_x[half:] + last_l
        own_bottom = rest[2][half:] + last_x + got_l[half:]
        return jnp.concatenate([own_top, own_bottom], axis=0)

    def flip(values, name):
        return lax.ppermute(values, name, FLIP)

    def gather(rows):
        return lax.all_gather(rows, SQUARE, axis=0, tiled=True)

    def low_dot(left, right):
        return dot_nn(left, right).astype(jnp.bfloat16)

    def body(
        tokens,
        gain_one,
        w_query,
        w_key,
        w_value,
        w_out,
        gain_two,
        w_gate,
        w_up,
        w_down,
        doc_ids,
        cotangent,
    ):
        for_twin, for_own = orders()
        halves_at, place = places()
        stacked = jnp.arange(4, dtype=jnp.int32)
        qkv_size = HEAD_V + 2 * FEAT
        head_size = qkv_size + HEAD_V
        own_tokens = trade(tokens)
        head_half = jnp.concatenate(
            [
                my_half(w_value, 1).T,
                my_half(w_query.T),
                my_half(w_key.T),
                my_half(w_out),
                jnp.broadcast_to(doc_ids.astype(jnp.bfloat16), (16, doc_ids.shape[1])),
            ],
            axis=0,
        )
        down_half, gate_half, up_half = my_half(w_down), my_half(w_gate.T), my_half(w_up.T)
        own_tokens = after(own_tokens, head_half, down_half, gate_half, up_half)
        inputs = own_tokens.astype(jnp.float32)
        normed_one, scale_one, low_one = norm_rows(inputs, gain_one)

        head_mine = trade(after(head_half, low_one))
        from_x, from_l, head_mine, own_grad = sync(
            flip(low_one, "x"), flip(low_one, "l"), head_mine, trade(after(cotangent, low_one))
        )
        grad_rows = gather(own_grad)
        half = low_one.shape[0] // 2
        qkv_other = over_y(head_mine[:qkv_size])
        d_top = flip(from_l[:half], "x")
        d_bottom = flip(from_x[half:], "l")
        stack_own = jnp.concatenate([d_top, d_bottom, from_x, from_l, low_one], axis=0)
        stack_own, qkv_other = sync(stack_own, qkv_other)
        stack_twin = flip(stack_own, "k")
        wo_other = over_y(after(head_mine[qkv_size:head_size], qkv_other))
        first, ends = bounds(head_mine[head_size].astype(jnp.int32))
        w_qkv = jnp.concatenate(
            [
                head_mine[:HEAD_V],
                qkv_other[:HEAD_V],
                head_mine[HEAD_V : HEAD_V + FEAT],
                qkv_other[HEAD_V : HEAD_V + FEAT],
                head_mine[HEAD_V + FEAT : qkv_size],
                qkv_other[HEAD_V + FEAT : qkv_size],
            ],
            axis=0,
        )
        stack_twin, w_qkv, first = sync(stack_twin, w_qkv, first)

        down_mine = trade(after(down_half, own_grad))
        qkv, mixed_heads, ratio, denom = attention_rows(
            first, halves_at, ends, stack_twin, stack_own, w_qkv
        )
        mixed_heads, down_mine, wo_other = sync(mixed_heads, down_mine, wo_other)
        wo = jnp.concatenate([head_mine[qkv_size:head_size], wo_other], axis=0)

        from_twin = flip(product_rows(for_twin, mixed_heads, wo), "k")
        down_other = over_y(down_mine)
        gate_mine = trade(after(gate_half, down_mine))
        (first_x, first_l), rest = scatter_first(
            product_rows(for_own, mixed_heads, wo), from_twin
        )
        got_x, got_l, down_other = sync(flip(first_x, "x"), flip(first_l, "l"), down_other)
        to_x, to_l = scatter_last(got_x, got_l, rest)
        attn_out = scatter_end(got_x, got_l, flip(to_x, "x"), flip(to_l, "l"), rest)
        attn_out, gate_mine = sync(attn_out, gate_mine)
        up_mine = trade(after(up_half, gate_mine))
        gate_other = over_y(gate_mine)

        residual = inputs + attn_out
        normed_two, scale_two, low_two = norm_rows(residual, gain_two)
        gathered_two = gather(low_two)
        wd = jnp.concatenate([down_mine, down_other], axis=0)
        grad_hidden = hidden_grad(down_mine, down_other, after(grad_rows, low_two, up_mine))
        up_other = over_y(up_mine)
        gathered_two, up_other, gate_other, grad_hidden = sync(
            gathered_two, up_other, gate_other, grad_hidden
        )

        weights = (gate_mine, up_mine, gate_other, up_other)
        *acts, parts_twin = ffn_rows(for_twin, gathered_two, grad_hidden, weights)
        from_twin = flip(parts_twin, "k")
        act_grad, hidden, parts_own = ffn_rows(
            for_own, gathered_two, grad_hidden, weights, tuple(acts)
        )
        unit_rows = {"gate": gathered_two, "up": gathered_two, "down": grad_rows}
        unit_at = {"gate": (0, 2, 4), "up": (1, 3, 4), "down": (0, 1, 2)}

        def other_part(name, *deps):
            _, piece, pieces = unit_at[name]
            acts = after(hidden if pieces == 2 else act_grad, *deps)
            return unit_grad(acts, piece, pieces, unit_rows[name])

        def y_total(name, arrived):
            piece, _, pieces = unit_at[name]
            acts = hidden if pieces == 2 else act_grad
            return all_y(unit_grad(acts, piece, pieces, unit_rows[name], arrived))

        (first_x, first_l), rest = scatter_first(parts_own, from_twin)
        down_part = other_part("down", first_x)
        down_y = over_y(down_part)
        gate_part = other_part("gate", down_part)
        up_part = other_part("up", gate_part)
        got_x, got_l, gate_part, up_part = sync(
            flip(first_x, "x"), flip(first_l, "l"), gate_part, up_part
        )
        to_x, to_l = scatter_last(got_x, got_l, rest)
        late_hidden = after(hidden, to_x)
        ffn_twin = product_rows(for_twin, late_hidden, wd, turned=True)
        ffn_own = product_rows(for_own, late_hidden, wd, turned=True)
        grad_normed_two = scatter_end(got_x, got_l, flip(to_x, "x"), flip(to_l, "l"), rest)
        grad_normed_two, down_y, ffn_twin, ffn_own = sync(
            grad_normed_two, down_y, ffn_twin, ffn_own
        )

        gate_y = over_y(gate_part)
        up_y = over_y(up_part)
        gain_two_part = jnp.sum(grad_normed_two * normed_two, axis=0)
        grad_resid = own_grad.astype(jnp.float32) + norm_back(
            grad_normed_two, normed_two, scale_two, gain_two
        )
        low_resid = grad_resid.astype(jnp.bfloat16)
        grad_attn_rows = gather(low_resid)
        down_total = y_total("down", after(down_y, low_resid))
        down_h = over_h(down_total)
        ffn_from_twin = flip(after(ffn_twin, low_resid), "k")
        (ffn_x, ffn_l), ffn_rest = scatter_first(ffn_own, ffn_from_twin)
        gate_total = y_total("gate", after(gate_y, down_total))
        gate_h = over_h(gate_total)
        up_total = y_total("up", after(up_y, gate_total))
        up_h = over_h(up_total)
        grad_attn_rows, up_total, ffn_x, ffn_l = sync(grad_attn_rows, up_total, ffn_x, ffn_l)

        grad_qkv = attention_back(
            first, place, ends, grad_attn_rows, wo, qkv, ratio, denom
        )
        grad_qkv, down_h, gate_h = sync(grad_qkv, down_h, gate_h)

        from_twin = flip(product_rows(stacked, grad_qkv, w_qkv), "k")
        one_own = product_rows(stacked + 4, grad_qkv, w_qkv)
        (first_x, first_l), rest = scatter_first(one_own, from_twin)
        head_part, head_other, gain_one_part = head_grads(
            after(grad_qkv, first_x),
            stack_twin,
            stack_own,
            mixed_heads,
            grad_attn_rows,
            w_qkv,
            gain_one,
        )
        head_y = over_y(head_other)
        down_total = after(down_total, head_other) + down_h
        down_back = over_owners(down_total)
        got_x, got_l, up_h = sync(flip(first_x, "x"), flip(first_l, "l"), up_h)
        to_x, to_l = scatter_last(got_x, got_l, rest)
        gain_grads = jnp.concatenate([gain_one_part, gain_two_part[None]], axis=0)
        gate_total = after(gate_total, to_x) + gate_h
        gate_back = over_owners(gate_total)
        grad_normed_one = scatter_end(got_x, got_l, flip(to_x, "x"), flip(to_l, "l"), rest)
        grad_normed_one, ffn_x, ffn_l = sync(grad_normed_one, ffn_x, ffn_l)

        grad_tokens = grad_resid + norm_back(grad_normed_one, normed_one, scale_one, gain_one)
        low_tokens = grad_tokens.astype(jnp.bfloat16)
        grad_tokens = trade(low_tokens)
        head_total = all_y((after(head_part, low_tokens) + head_y).astype(jnp.bfloat16))
        head_h = over_h(head_total)
        flags = jnp.stack(
            [lax.axis_index("y") % 2, (lax.axis_index("k") == lax.axis_index("h")).astype(jnp.int32)]
        )

        def spread(total, back):
            return total, to_twin(total), back, to_twin(back)

        down_parts, gate_parts = spread(down_total, down_back), spread(gate_total, gate_back)
        grad_tokens, head_h, up_total, got_x, got_l, *parts = sync(
            grad_tokens,
            head_h,
            up_total,
            flip(ffn_x, "x"),
            flip(ffn_l, "l"),
            *down_parts,
            *gate_parts,
        )
        head_total = head_total + head_h
        head_back, head_cross = over_owners(head_total), across(head_total)
        up_total = up_total + up_h
        up_back = over_owners(up_total)
        to_x, to_l = scatter_last(got_x, got_l, ffn_rest)
        last_x, last_l, down_grad, gate_grad, up_back = sync(
            flip(to_x, "x"),
            flip(to_l, "l"),
            finish_unit(flags, *parts[:4]),
            finish_unit(flags, *parts[4:]),
            up_back,
        )
        ffn_out = scatter_end(got_x, got_l, last_x, last_l, ffn_rest)
        block_out = trade((residual + ffn_out).astype(jnp.bfloat16))
        up_grad = finish_unit(flags, *spread(up_total, up_back))
        query_grad, key_grad, value_grad, out_grad = finish_head(
            flags, head_total, to_twin(head_total), head_back, head_cross
        )
        for name in ("k", "x", "l", "h"):
            gain_grads = gain_grads + flip(gain_grads, name)
        step = 1
        while step < y_size:
            gain_grads = gain_grads + lax.ppermute(
                gain_grads, "y", [(i, i ^ step) for i in range(y_size)]
            )
            step *= 2

        return (
            block_out,
            grad_tokens.astype(jnp.float32),
            gain_grads[0],
            query_grad.T,
            key_grad.T,
            value_grad,
            out_grad,
            gain_grads[1],
            gate_grad.T,
            up_grad.T,
            down_grad,
        )

    return body


def solution(mesh):
    dp_size, tensor_size = mesh.devices.shape
    fine = Mesh(mesh.devices.reshape(dp_size // 2, 2, 2, 2, tensor_size // 4), ALL_AXES)
    rows = P(ALL_AXES, None)
    shard = ("h", "l", "x")
    in_specs = (
        rows,
        P(),
        P(None, shard),
        P(None, shard),
        P(None, shard),
        P(shard, None),
        P(),
        P(None, shard),
        P(None, shard),
        P(shard, None),
        P(("y", "k"), None),
        rows,
    )
    out_specs = (
        rows,
        rows,
        P(),
        P(None, shard),
        P(None, shard),
        P(None, shard),
        P(shard, None),
        P(),
        P(None, shard),
        P(None, shard),
        P(shard, None),
    )
    return jax.shard_map(
        make_body(dp_size // 2), mesh=fine, in_specs=in_specs, out_specs=out_specs, check_vma=False
    )
```

```python
import functools

import jax
import jax.numpy as jnp
from jax import lax
from jax.experimental import pallas as pl
from jax.experimental.pallas import tpu as pltpu
from jax.sharding import Mesh
from jax.sharding import PartitionSpec as P

FEAT = 16
HEAD_V = 128
EPS = 1e-05
VALUES = 2 * HEAD_V
FEATS = 2 * FEAT
NO_COST = pl.CostEstimate(flops=1, bytes_accessed=1, transcendentals=0)

ALL_AXES = ("y", "k", "h", "l", "x")
FLIP = [(0, 1), (1, 0)]
SQUARE = ("k", "l", "x")


def norm_rows(values, gain_vec):
    row_scale = lax.rsqrt(jnp.mean(values * values, axis=-1, keepdims=True) + EPS)
    normed = values * row_scale
    return (normed, row_scale, (normed * gain_vec).astype(jnp.bfloat16))


def norm_back(grad_normed, normed, row_scale, gain_vec):
    weighted = grad_normed * gain_vec
    inner_mean = jnp.mean(weighted * normed, axis=-1, keepdims=True)
    return row_scale * (weighted - normed * inner_mean)


def dot_nn(left_mat, right_mat):
    return jnp.dot(left_mat, right_mat, preferred_element_type=jnp.float32)


def dot_tn(left_mat, right_mat):
    return lax.dot_general(
        left_mat, right_mat, (((0,), (0,)), ((), ())), preferred_element_type=jnp.float32
    )


def dot_nt(left_mat, right_mat):
    return lax.dot_general(
        left_mat, right_mat, (((1,), (1,)), ((), ())), preferred_element_type=jnp.float32
    )


def head_lanes(values, head):
    lane = lax.broadcasted_iota(jnp.int32, values.shape, 1)
    return jnp.where((lane >= head * FEAT) & (lane < (head + 1) * FEAT), values, jnp.zeros_like(values))

def scores(query, keys, ends_ref, i, j, block):
    score = dot_nt(query, keys) * 0.25
    t = i * block + lax.broadcasted_iota(jnp.int32, score.shape, 0)
    u = j * block + lax.broadcasted_iota(jnp.int32, score.shape, 1)
    ends = ends_ref[:, pl.ds(pl.multiple_of(jnp.minimum(j, i) * block, block), block)]
    allowed = (t >= u) & (t <= ends)
    return score, allowed, jnp.where(allowed, 1.0 + score + 0.5 * score * score, 0.0)

def forward_kernel(
    first_ref,
    twin_at_ref,
    own_at_ref,
    is_own_ref,
    twin_ref,
    own_ref,
    weight_ref,
    ends_ref,
    qkv_ref,
    mixed_ref,
    ratio_ref,
    denom_ref,
    key_ref,
    numer_ref,
    sum_ref,
):
    i = pl.program_id(0)
    block = own_ref.shape[0]
    here = pl.ds(pl.multiple_of(i * block, block), block)

    def project(rows_ref):
        qkv_ref[here] = dot_nt(rows_ref[...], weight_ref[...]).astype(jnp.bfloat16)

    pl.when(is_own_ref[i] == 1)(lambda: project(own_ref))
    pl.when(is_own_ref[i] == 0)(lambda: project(twin_ref))
    key_ref[here] = qkv_ref[here, VALUES + FEATS :]
    query = qkv_ref[here, VALUES : VALUES + FEATS]
    own = [head_lanes(query, head) for head in range(2)]
    numer_ref[...] = jnp.zeros_like(numer_ref)
    sum_ref[...] = jnp.zeros_like(sum_ref)

    def step(pair, carry):
        for head in range(2):
            columns = pl.ds(head * HEAD_V, HEAD_V)
            folded, numer = None, None
            for j in (first_ref[i] + 2 * pair, first_ref[i] + 2 * pair + 1):
                there = pl.ds(pl.multiple_of(jnp.minimum(j, i) * block, block), block)
                _, _, kernel = scores(own[head], key_ref[there], ends_ref, i, j, block)
                parts = [kernel[:, c * 128 : (c + 1) * 128] for c in range(block // 128)]
                part = dot_nn(kernel.astype(jnp.bfloat16), qkv_ref[there, columns])
                folded = sum(parts) if folded is None else folded + sum(parts)
                numer = part if numer is None else numer + part
            sum_ref[:, pl.ds(head * 128, 128)] += folded
            numer_ref[:, columns] += numer
        return carry

    lax.fori_loop(0, (i + 2 - first_ref[i]) // 2, step, 0)
    for head in range(2):
        columns = pl.ds(head * HEAD_V, HEAD_V)
        denom = jnp.sum(sum_ref[:, pl.ds(head * 128, 128)], axis=1, keepdims=True)
        ratio = numer_ref[:, columns] / denom
        mixed_ref[:, columns] = ratio.astype(jnp.bfloat16)
        ratio_ref[:, columns] = ratio
        denom_ref[:, columns] = jnp.broadcast_to(denom, ratio.shape)

def attention_rows(first, places, ends, twin, own, weight):
    half_rows, model = own.shape
    group_rows = 2 * half_rows
    block = group_rows // 8
    width = VALUES + 2 * FEATS

    def by_rows(columns):
        return pl.BlockSpec((block, columns), lambda i, *_: (i, 0))

    def whole(shape):
        return pl.BlockSpec(shape, lambda i, *_: (0, 0))

    return pl.pallas_call(
        forward_kernel,
        out_shape=[
            jax.ShapeDtypeStruct((group_rows, width), jnp.bfloat16),
            jax.ShapeDtypeStruct((group_rows, VALUES), jnp.bfloat16),
            jax.ShapeDtypeStruct((group_rows, VALUES), jnp.float32),
            jax.ShapeDtypeStruct((group_rows, VALUES), jnp.float32),
        ],
        grid_spec=pltpu.PrefetchScalarGridSpec(
            num_scalar_prefetch=4,
            grid=(8,),
            in_specs=[
                pl.BlockSpec((block, model), lambda i, f, twin_at, own_at, s: (twin_at[i], 0)),
                pl.BlockSpec((block, model), lambda i, f, twin_at, own_at, s: (own_at[i], 0)),
                whole((width, model)),
                whole((1, group_rows)),
            ],
            out_specs=[
                whole((group_rows, width)),
                by_rows(VALUES),
                by_rows(VALUES),
                by_rows(VALUES),
            ],
            scratch_shapes=[
                pltpu.VMEM((group_rows, FEATS), jnp.bfloat16),
                pltpu.VMEM((block, VALUES), jnp.float32),
                pltpu.VMEM((block, 256), jnp.float32),
            ],
        ),
        compiler_params=pltpu.CompilerParams(vmem_limit_bytes=32 << 20),
        cost_estimate=NO_COST,
        name="attention_rows",
    )(first, *places, twin, own, weight, ends)


def backward_kernel(
    first_ref,
    place_ref,
    attn_ref,
    weight_ref,
    qkv_ref,
    ratio_ref,
    denom_ref,
    ends_ref,
    grad_ref,
    key_ref,
    key_sum,
    value_sum,
    query_sum,
):
    i = pl.program_id(0)
    block = attn_ref.shape[0]
    here = pl.ds(pl.multiple_of(i * block, block), block)
    @pl.when(i == 0)
    def _():
        key_ref[...] = qkv_ref[:, VALUES + FEATS:]
        key_sum[...] = jnp.zeros_like(key_sum)
        value_sum[...] = jnp.zeros_like(value_sum)
    mixed_grad = dot_nt(attn_ref[...], weight_ref[...]).astype(jnp.bfloat16).astype(jnp.float32)
    query = qkv_ref[here, VALUES : VALUES + FEATS]
    own = [head_lanes(query, head) for head in range(2)]
    numer_grads, denom_grads = [], []
    for head in range(2):
        columns = pl.ds(head * HEAD_V, HEAD_V)
        grad = mixed_grad[:, head * HEAD_V : (head + 1) * HEAD_V]
        denom = denom_ref[:, columns]
        numer_grads.append((grad / denom).astype(jnp.bfloat16))
        denom_grads.append(-jnp.sum(grad * ratio_ref[:, columns], axis=1, keepdims=True) / denom[:, :1])
    query_sum[...] = jnp.zeros_like(query_sum)

    def step(j, carry):
        there = pl.ds(pl.multiple_of(j * block, block), block)
        keys = key_ref[there]
        key_grads = None
        for head in range(2):
            columns = pl.ds(head * HEAD_V, HEAD_V)
            score, allowed, kernel = scores(own[head], keys, ends_ref, i, j, block)
            kernel_grad = dot_nt(numer_grads[head], qkv_ref[there, columns]) + denom_grads[head]
            score_grad = jnp.where(allowed, kernel_grad * (1.0 + score), 0.0).astype(jnp.bfloat16)
            query_sum[:, pl.ds(head * 128, FEATS)] += dot_nn(score_grad, keys)
            key_grad = dot_tn(score_grad, own[head])
            key_grads = key_grad if key_grads is None else key_grads + key_grad
            value_sum[there, columns] += dot_tn(kernel.astype(jnp.bfloat16), numer_grads[head])
        key_sum[there] += key_grads
        return carry

    lax.fori_loop(first_ref[i], i + 1, step, 0)
    totals = [query_sum[:, pl.ds(head * 128, FEATS)] for head in range(2)]
    query_grad = (head_lanes(totals[0], 0) + head_lanes(totals[1], 1)) * 0.25
    placed = pl.ds(pl.multiple_of(place_ref[i] * block, block), block)
    grad_ref[placed, VALUES : VALUES + FEATS] = query_grad.astype(jnp.bfloat16)

    @pl.when(i == pl.num_programs(0) - 1)
    def _():
        def store(j, carry):
            there = pl.ds(pl.multiple_of(j * block, block), block)
            placed = pl.ds(pl.multiple_of(place_ref[j] * block, block), block)
            grad_ref[placed, :VALUES] = value_sum[there].astype(jnp.bfloat16)
            grad_ref[placed, VALUES + FEATS :] = (key_sum[there] * 0.25).astype(jnp.bfloat16)
            return carry

        lax.fori_loop(0, pl.num_programs(0), store, 0)

def attention_back(first, place, ends, attn_rows, weight, qkv, ratio, denom):
    group_rows, model = attn_rows.shape
    block = group_rows // 8
    width = VALUES + 2 * FEATS

    def by_rows(columns):
        return pl.BlockSpec((block, columns), lambda i, *_: (i, 0))

    def whole(shape):
        return pl.BlockSpec(shape, lambda i, *_: (0, 0))

    return pl.pallas_call(
        backward_kernel,
        out_shape=jax.ShapeDtypeStruct((group_rows, width), jnp.bfloat16),
        grid_spec=pltpu.PrefetchScalarGridSpec(
            num_scalar_prefetch=2,
            grid=(8,),
            in_specs=[
                by_rows(model),
                whole((VALUES, model)),
                whole((group_rows, width)),
                by_rows(VALUES),
                by_rows(VALUES),
                whole((1, group_rows)),
            ],
            out_specs=whole((group_rows, width)),
            scratch_shapes=[
                pltpu.VMEM((group_rows, FEATS), jnp.bfloat16),
                pltpu.VMEM((group_rows, FEATS), jnp.float32),
                pltpu.VMEM((group_rows, VALUES), jnp.float32),
                pltpu.VMEM((block, 256), jnp.float32),
            ],
        ),
        compiler_params=pltpu.CompilerParams(vmem_limit_bytes=40 << 20),
        cost_estimate=NO_COST,
        name="attention_back",
    )(first, place, attn_rows, weight, qkv, ratio, denom, ends)


def bounds(doc_row):
    group_rows = doc_row.shape[0]; block = group_rows // 8
    ends = jnp.sum(doc_row[:, None] <= doc_row[None, :], axis=0, dtype=jnp.int32) - 1
    starts = block * jnp.arange(8, dtype=jnp.int32)
    first = jnp.sum(ends[block - 1 :: block][None, :] < starts[:, None], axis=1, dtype=jnp.int32)
    return first, ends.reshape(1, group_rows)


def ffn_kernel(pieces, order_ref, rows_ref, grad_ref, *refs):
    weights = refs[:4]
    act_grad_ref, hidden_ref, part_ref, held, sems = refs[-5:]

    @pl.when(pl.program_id(0) == 0)
    def _():
        copies = [
            pltpu.make_async_copy(ref, held.at[pl.ds(i * pieces, pieces)], sems.at[i])
            for i, ref in enumerate(weights)
        ]
        for copy in copies:
            copy.start()

    rows = rows_ref[...]
    for half in range(2):
        at = 2 * half * pieces

        @pl.when(pl.program_id(0) == 0)
        def _(half=half):
            for i in (2 * half, 2 * half + 1):
                pltpu.make_async_copy(
                    weights[i], held.at[pl.ds(i * pieces, pieces)], sems.at[i]
                ).wait()

        gate = dot_nt(held[pl.ds(at, pieces)], rows)
        up = dot_nt(held[pl.ds(at + pieces, pieces)], rows)
        grad = grad_ref[pl.ds(half * pieces, pieces)]
        sigmoid = jax.nn.sigmoid(gate)
        act = gate * sigmoid
        hidden_ref[pl.ds(half * pieces, pieces)] = (act * up).astype(jnp.bfloat16)
        act_grad_ref[pl.ds(at, pieces)] = (
            grad * up * (sigmoid * (1.0 + gate * (1.0 - sigmoid)))
        ).astype(jnp.bfloat16)
        act_grad_ref[pl.ds(at + pieces, pieces)] = (grad * act).astype(jnp.bfloat16)
    part_ref[...] = dot_tn(act_grad_ref[...], held[...]).astype(jnp.bfloat16)


def ffn_rows(order, rows, grad_hidden, weights, earlier=()):
    group_rows, model = rows.shape
    pieces = weights[0].shape[0]
    block = group_rows // 8
    blocks = order.shape[0]
    anywhere = pl.BlockSpec(memory_space=pl.ANY)
    return pl.pallas_call(
        functools.partial(ffn_kernel, pieces),
        out_shape=[
            jax.ShapeDtypeStruct((4 * pieces, group_rows), jnp.bfloat16),
            jax.ShapeDtypeStruct((2 * pieces, group_rows), jnp.bfloat16),
            jax.ShapeDtypeStruct((blocks * block, model), jnp.bfloat16),
        ],
        grid_spec=pltpu.PrefetchScalarGridSpec(
            num_scalar_prefetch=1,
            grid=(blocks,),
            in_specs=[
                pl.BlockSpec((block, model), lambda i, o: (o[i], 0)),
                pl.BlockSpec((2 * pieces, block), lambda i, o: (0, o[i])),
                *[anywhere] * (4 + len(earlier)),
            ],
            out_specs=[
                pl.BlockSpec((4 * pieces, block), lambda i, o: (0, o[i])),
                pl.BlockSpec((2 * pieces, block), lambda i, o: (0, o[i])),
                pl.BlockSpec((block, model), lambda i, o: (i, 0)),
            ],
            scratch_shapes=[
                pltpu.VMEM((4 * pieces, model), jnp.bfloat16),
                pltpu.SemaphoreType.DMA((4,)),
            ],
        ),
        input_output_aliases={7 + i: i for i in range(len(earlier))},
        compiler_params=pltpu.CompilerParams(vmem_limit_bytes=44 << 20),
        cost_estimate=NO_COST,
        name="ffn_rows",
    )(order, rows, grad_hidden, *weights, *earlier)


def product_kernel(turned, order_ref, rows_ref, weight_ref, part_ref):
    product = dot_tn if turned else dot_nn
    part_ref[...] = product(rows_ref[...], weight_ref[...]).astype(jnp.bfloat16)


def product_rows(order, rows, weight, turned=False):
    group_rows = rows.shape[1 if turned else 0]
    depth, model = weight.shape
    block = group_rows // 8
    blocks = order.shape[0]
    if turned:
        rows_spec = pl.BlockSpec((depth, block), lambda i, o: (0, o[i]))
    else:
        rows_spec = pl.BlockSpec((block, depth), lambda i, o: (o[i], 0))
    return pl.pallas_call(
        functools.partial(product_kernel, turned),
        out_shape=jax.ShapeDtypeStruct((blocks * block, model), jnp.bfloat16),
        grid_spec=pltpu.PrefetchScalarGridSpec(
            num_scalar_prefetch=1,
            grid=(blocks,),
            in_specs=[rows_spec, pl.BlockSpec((depth, model), lambda i, o: (0, 0))],
            out_specs=pl.BlockSpec((block, model), lambda i, o: (i, 0)),
        ),
        compiler_params=pltpu.CompilerParams(vmem_limit_bytes=24 << 20),
        cost_estimate=NO_COST,
        name="product_rows",
    )(order, rows, weight)


def unit_kernel(with_arrived, acts_ref, rows_ref, *refs):
    total = dot_nn(acts_ref[...], rows_ref[...])
    if with_arrived:
        total = total + refs[0][...]
    refs[-1][...] = total.astype(jnp.bfloat16)


def unit_grad(acts, piece, pieces, rows, arrived=None):
    units = acts.shape[0] // pieces
    group_rows, model = rows.shape
    columns = model // 4
    part = pl.BlockSpec((units, columns), lambda i: (0, i))
    return pl.pallas_call(
        functools.partial(unit_kernel, arrived is not None),
        out_shape=jax.ShapeDtypeStruct((units, model), jnp.bfloat16),
        grid=(4,),
        in_specs=[
            pl.BlockSpec((units, group_rows), lambda i: (piece, 0)),
            pl.BlockSpec((group_rows, columns), lambda i: (0, i)),
            *([] if arrived is None else [part]),
        ],
        out_specs=part,
        compiler_params=pltpu.CompilerParams(vmem_limit_bytes=24 << 20),
        cost_estimate=NO_COST,
        name="unit_grad",
    )(acts, rows, *([] if arrived is None else [arrived]))


def hidden_kernel(mine_ref, other_ref, rows_ref, grad_ref):
    half = mine_ref.shape[0]
    grad_ref[pl.ds(0, half)] = dot_nt(mine_ref[...], rows_ref[...])
    grad_ref[pl.ds(half, half)] = dot_nt(other_ref[...], rows_ref[...])


def hidden_grad(mine, other, rows):
    half, model = mine.shape
    group_rows = rows.shape[0]
    block = group_rows // 4
    weight = pl.BlockSpec((half, model), lambda i: (0, 0))
    return pl.pallas_call(
        hidden_kernel,
        out_shape=jax.ShapeDtypeStruct((2 * half, group_rows), jnp.float32),
        grid=(4,),
        in_specs=[weight, weight, pl.BlockSpec((block, model), lambda i: (i, 0))],
        out_specs=pl.BlockSpec((2 * half, block), lambda i: (0, i)),
        compiler_params=pltpu.CompilerParams(vmem_limit_bytes=28 << 20),
        cost_estimate=NO_COST,
        name="hidden_grad",
    )(mine, other, rows)


def head_kernel(
    qkv_ref, twin_ref, own_ref, mixed_ref, attn_ref, weight_ref, gain_ref, mine_ref, other_ref, sum_ref
):
    half = twin_ref.shape[0]
    qkv = dot_tn(qkv_ref[pl.ds(0, half)], twin_ref[...]) + dot_tn(
        qkv_ref[pl.ds(half, half)], own_ref[...]
    )
    out = dot_tn(mixed_ref[...], attn_ref[...])
    gain_grad = jnp.sum(qkv * weight_ref[...].astype(jnp.float32), axis=0, keepdims=True)
    sum_ref[...] = gain_grad / gain_ref[...]
    for which, ref in enumerate((mine_ref, other_ref)):
        at = VALUES + which * FEAT
        ref[pl.ds(0, HEAD_V)] = qkv[which * HEAD_V : (which + 1) * HEAD_V].astype(ref.dtype)
        ref[pl.ds(HEAD_V, FEAT)] = qkv[at : at + FEAT].astype(ref.dtype)
        ref[pl.ds(HEAD_V + FEAT, FEAT)] = qkv[at + FEATS : at + FEATS + FEAT].astype(ref.dtype)
        ref[pl.ds(HEAD_V + 2 * FEAT, HEAD_V)] = out[which * HEAD_V : (which + 1) * HEAD_V].astype(
            ref.dtype
        )


def head_grads(qkv, twin, own, mixed, attn_rows, weight, gain):
    group_rows, model = attn_rows.shape
    columns = model // 4
    size = 2 * HEAD_V + 2 * FEAT

    def whole(values):
        return pl.BlockSpec(values.shape, lambda i: (0, 0))

    def part(rows):
        return pl.BlockSpec((rows, columns), lambda i: (0, i))

    return pl.pallas_call(
        head_kernel,
        out_shape=[
            jax.ShapeDtypeStruct((size, model), jnp.float32),
            jax.ShapeDtypeStruct((size, model), jnp.bfloat16),
            jax.ShapeDtypeStruct((1, model), jnp.float32),
        ],
        grid=(4,),
        in_specs=[
            whole(qkv),
            part(group_rows // 2),
            part(group_rows // 2),
            whole(mixed),
            part(group_rows),
            part(weight.shape[0]),
            part(1),
        ],
        out_specs=[part(size), part(size), part(1)],
        compiler_params=pltpu.CompilerParams(vmem_limit_bytes=32 << 20),
        cost_estimate=NO_COST,
        name="head_grads",
    )(qkv, twin, own, mixed, attn_rows, weight, gain.reshape(1, model))


def chosen(flags_ref, own_ref, twin_ref):
    return jnp.where(flags_ref[1] == 1, own_ref[...], twin_ref[...]).astype(jnp.float32)


def finish_kernel(flags_ref, mine_ref, mine_twin_ref, theirs_ref, theirs_twin_ref, grad_ref):
    half = mine_ref.shape[0]
    mine, theirs = pl.ds(flags_ref[0] * half, half), pl.ds((1 - flags_ref[0]) * half, half)
    grad_ref[mine] = chosen(flags_ref, mine_ref, mine_twin_ref)
    grad_ref[theirs] = chosen(flags_ref, theirs_ref, theirs_twin_ref)


def finish_unit(flags, *parts):
    half, model = parts[0].shape
    columns = model // 4
    part = pl.BlockSpec((half, columns), lambda i, f: (0, i))
    return pl.pallas_call(
        finish_kernel,
        out_shape=jax.ShapeDtypeStruct((2 * half, model), jnp.float32),
        grid_spec=pltpu.PrefetchScalarGridSpec(
            num_scalar_prefetch=1,
            grid=(4,),
            in_specs=[part] * 4,
            out_specs=pl.BlockSpec((2 * half, columns), lambda i, f: (0, i)),
        ),
        compiler_params=pltpu.CompilerParams(vmem_limit_bytes=24 << 20),
        cost_estimate=NO_COST,
        name="finish_unit",
    )(flags, *parts)


def finish_head_kernel(
    flags_ref, mine_ref, mine_twin_ref, theirs_ref, theirs_twin_ref, query_ref, key_ref, value_ref, out_ref
):
    halves = (
        (flags_ref[0], chosen(flags_ref, mine_ref, mine_twin_ref)),
        (1 - flags_ref[0], chosen(flags_ref, theirs_ref, theirs_twin_ref)),
    )
    for at, grads in halves:
        features = pl.ds(pl.multiple_of(at * FEAT, FEAT), FEAT)
        values = pl.ds(pl.multiple_of(at * HEAD_V, HEAD_V), HEAD_V)
        value_ref[:, values] = grads[:HEAD_V].T
        query_ref[features] = grads[HEAD_V : HEAD_V + FEAT]
        key_ref[features] = grads[HEAD_V + FEAT : HEAD_V + 2 * FEAT]
        out_ref[values] = grads[HEAD_V + 2 * FEAT :]


def finish_head(flags, *parts):
    size, model = parts[0].shape
    columns = model // 4

    def part(rows):
        return pl.BlockSpec((rows, columns), lambda i, f: (0, i))

    return pl.pallas_call(
        finish_head_kernel,
        out_shape=[
            jax.ShapeDtypeStruct((FEATS, model), jnp.float32),
            jax.ShapeDtypeStruct((FEATS, model), jnp.float32),
            jax.ShapeDtypeStruct((model, VALUES), jnp.float32),
            jax.ShapeDtypeStruct((VALUES, model), jnp.float32),
        ],
        grid_spec=pltpu.PrefetchScalarGridSpec(
            num_scalar_prefetch=1,
            grid=(4,),
            in_specs=[part(size)] * 4,
            out_specs=[
                part(FEATS),
                part(FEATS),
                pl.BlockSpec((columns, VALUES), lambda i, f: (i, 0)),
                part(VALUES),
            ],
        ),
        compiler_params=pltpu.CompilerParams(vmem_limit_bytes=24 << 20),
        cost_estimate=NO_COST,
        name="finish_head",
    )(flags, *parts)


def sync(*values):
    return lax.optimization_barrier(values)


def after(value, *others):
    return lax.optimization_barrier((value, *others))[0]


def make_body(y_size):
    y_pairs = [(i, i ^ 1) for i in range(y_size)]
    owner_y_pairs = [(i * 4 + kh, (i ^ 1) * 4 + kh) for i in range(y_size) for kh in (0, 3)]

    cross_pairs = [(i * 4 + kh, (i ^ 1) * 4 + (kh ^ 2)) for i in range(y_size) for kh in (0, 3)]

    def trade(values):
        return lax.ppermute(values, ("k", "h"), [(0, 0), (1, 2), (2, 1), (3, 3)])

    def over_y(values):
        return lax.ppermute(values, "y", y_pairs)

    def over_h(values):
        return lax.ppermute(values, ("k", "h"), [(1, 0), (2, 3)])

    def over_owners(values):
        return lax.ppermute(values, ("y", "k", "h"), owner_y_pairs)

    def to_twin(values):
        return lax.ppermute(values, ("k", "h"), [(0, 2), (3, 1)])

    def across(values):
        return lax.ppermute(values, ("y", "k", "h"), cross_pairs)

    def all_y(total):
        step = 2
        while step < y_size:
            total = total + lax.ppermute(total, "y", [(i, i ^ step) for i in range(y_size)])
            step *= 2
        return total

    def my_half(own, axis=0):
        half = own.shape[axis] // 2
        return lax.dynamic_slice_in_dim(own, (lax.axis_index("y") % 2) * half, half, axis)

    def orders():
        k, l, x = (lax.axis_index(name) for name in SQUARE)
        chips = jnp.array([3, 1, 2, 0], jnp.int32) ^ (2 * l + x)
        return (chips + 4 * (1 - k), chips + 4 * k)

    def places():
        k, l, x = (lax.axis_index(name) for name in SQUARE)
        index = jnp.arange(8, dtype=jnp.int32)

        def slot(block):
            chip = (block % 4) ^ (2 * l + x)
            return jnp.where((chip == 0) | (chip == 3), 3 - chip, chip)

        first_twin = 4 * (1 - k)
        twin_at = slot(jnp.clip(index, first_twin, first_twin + 3))
        own_at = slot(jnp.clip(index, 4 * k, 4 * k + 3))
        is_own = (index // 4 == k).astype(jnp.int32)
        return (twin_at, own_at, is_own), slot(index) + 4 * is_own

    def low(*values):
        return jnp.concatenate(values, axis=0).astype(jnp.bfloat16)

    def scatter_first(mine, from_twin):
        rows = mine.shape[0] // 4
        half = rows // 2

        def chip(start, stop):
            return mine[start:stop].astype(jnp.float32) + from_twin[start:stop]

        first_x = low(chip(0, half), chip(rows, rows + half))
        first_l = low(chip(half, rows), chip(2 * rows + half, 3 * rows))
        rest = (
            chip(rows + half, 2 * rows),
            chip(2 * rows, 2 * rows + half),
            chip(3 * rows, 4 * rows),
        )
        return sync(first_x, first_l), rest

    def scatter_last(got_x, got_l, rest):
        half = got_x.shape[0] // 2
        return sync(low(rest[0] + got_l[:half]), low(rest[1] + got_x[:half]))

    def scatter_end(got_x, got_l, last_x, last_l, rest):
        half = got_x.shape[0] // 2
        own_top = rest[2][:half] + got_x[half:] + last_l
        own_bottom = rest[2][half:] + last_x + got_l[half:]
        return jnp.concatenate([own_top, own_bottom], axis=0)

    def flip(values, name):
        return lax.ppermute(values, name, FLIP)

    def gather(rows):
        return lax.all_gather(rows, SQUARE, axis=0, tiled=True)

    def low_dot(left, right):
        return dot_nn(left, right).astype(jnp.bfloat16)

    def body(
        tokens,
        gain_one,
        w_query,
        w_key,
        w_value,
        w_out,
        gain_two,
        w_gate,
        w_up,
        w_down,
        doc_ids,
        cotangent,
    ):
        for_twin, for_own = orders()
        halves_at, place = places()
        stacked = jnp.arange(4, dtype=jnp.int32)
        qkv_size = HEAD_V + 2 * FEAT
        head_size = qkv_size + HEAD_V
        own_tokens = trade(tokens)
        head_half = jnp.concatenate(
            [
                my_half(w_value, 1).T,
                my_half(w_query.T),
                my_half(w_key.T),
                my_half(w_out),
                jnp.broadcast_to(doc_ids.astype(jnp.bfloat16), (16, doc_ids.shape[1])),
            ],
            axis=0,
        )
        down_half, gate_half, up_half = my_half(w_down), my_half(w_gate.T), my_half(w_up.T)
        own_tokens = after(own_tokens, head_half, down_half, gate_half, up_half)
        inputs = own_tokens.astype(jnp.float32)
        normed_one, scale_one, low_one = norm_rows(inputs, gain_one)

        head_mine = trade(after(head_half, low_one))
        from_x, from_l, head_mine, own_grad = sync(
            flip(low_one, "x"), flip(low_one, "l"), head_mine, trade(after(cotangent, low_one))
        )
        grad_rows = gather(own_grad)
        half = low_one.shape[0] // 2
        qkv_other = over_y(head_mine[:qkv_size])
        d_top = flip(from_l[:half], "x")
        d_bottom = flip(from_x[half:], "l")
        stack_own = jnp.concatenate([d_top, d_bottom, from_x, from_l, low_one], axis=0)
        stack_own, qkv_other = sync(stack_own, qkv_other)
        stack_twin = flip(stack_own, "k")
        wo_other = over_y(after(head_mine[qkv_size:head_size], qkv_other))
        first, ends = bounds(head_mine[head_size].astype(jnp.int32))
        w_qkv = jnp.concatenate(
            [
                head_mine[:HEAD_V],
                qkv_other[:HEAD_V],
                head_mine[HEAD_V : HEAD_V + FEAT],
                qkv_other[HEAD_V : HEAD_V + FEAT],
                head_mine[HEAD_V + FEAT : qkv_size],
                qkv_other[HEAD_V + FEAT : qkv_size],
            ],
            axis=0,
        )
        stack_twin, w_qkv, first = sync(stack_twin, w_qkv, first)

        down_mine = trade(after(down_half, own_grad))
        qkv, mixed_heads, ratio, denom = attention_rows(
            first, halves_at, ends, stack_twin, stack_own, w_qkv
        )
        mixed_heads, wo_other = sync(mixed_heads, wo_other)
        wo = jnp.concatenate([head_mine[qkv_size:head_size], wo_other], axis=0)

        from_twin = flip(product_rows(for_twin, mixed_heads, wo), "k")
        from_twin, down_mine = sync(from_twin, down_mine)
        down_other = over_y(down_mine)
        gate_mine = trade(after(gate_half, mixed_heads))
        (first_x, first_l), rest = scatter_first(
            product_rows(for_own, mixed_heads, wo), from_twin
        )
        got_x, got_l, down_other = sync(flip(first_x, "x"), flip(first_l, "l"), down_other)
        to_x, to_l = scatter_last(got_x, got_l, rest)
        attn_out = scatter_end(got_x, got_l, flip(to_x, "x"), flip(to_l, "l"), rest)
        attn_out, gate_mine = sync(attn_out, gate_mine)
        up_mine = trade(after(up_half, gate_mine))
        gate_other = over_y(gate_mine)

        residual = inputs + attn_out
        normed_two, scale_two, low_two = norm_rows(residual, gain_two)
        gathered_two = gather(low_two)
        wd = jnp.concatenate([down_mine, down_other], axis=0)
        grad_hidden = hidden_grad(down_mine, down_other, after(grad_rows, low_two, up_mine))
        up_other = over_y(up_mine)
        gathered_two, up_other, gate_other, grad_hidden = sync(
            gathered_two, up_other, gate_other, grad_hidden
        )

        weights = (gate_mine, up_mine, gate_other, up_other)
        *acts, parts_twin = ffn_rows(for_twin, gathered_two, grad_hidden, weights)
        from_twin = flip(parts_twin, "k")
        act_grad, hidden, parts_own = ffn_rows(
            for_own, gathered_two, grad_hidden, weights, tuple(acts)
        )
        unit_rows = {"gate": gathered_two, "up": gathered_two, "down": grad_rows}
        unit_at = {"gate": (0, 2, 4), "up": (1, 3, 4), "down": (0, 1, 2)}

        def other_part(name, *deps):
            _, piece, pieces = unit_at[name]
            acts = after(hidden if pieces == 2 else act_grad, *deps)
            return unit_grad(acts, piece, pieces, unit_rows[name])

        def y_total(name, arrived):
            piece, _, pieces = unit_at[name]
            acts = hidden if pieces == 2 else act_grad
            return all_y(unit_grad(acts, piece, pieces, unit_rows[name], arrived))

        (first_x, first_l), rest = scatter_first(parts_own, from_twin)
        down_part = other_part("down", first_x)
        down_y = over_y(down_part)
        gate_part = other_part("gate", down_part)
        up_part = other_part("up", gate_part)
        got_x, got_l, gate_part, up_part = sync(
            flip(first_x, "x"), flip(first_l, "l"), gate_part, up_part
        )
        to_x, to_l = scatter_last(got_x, got_l, rest)
        late_hidden = after(hidden, to_x)
        ffn_twin = product_rows(for_twin, late_hidden, wd, turned=True)
        ffn_own = product_rows(for_own, late_hidden, wd, turned=True)
        grad_normed_two = scatter_end(got_x, got_l, flip(to_x, "x"), flip(to_l, "l"), rest)
        grad_normed_two, down_y, ffn_twin, ffn_own = sync(
            grad_normed_two, down_y, ffn_twin, ffn_own
        )

        gate_y = over_y(gate_part)
        up_y = over_y(up_part)
        gain_two_part = jnp.sum(grad_normed_two * normed_two, axis=0)
        grad_resid = own_grad.astype(jnp.float32) + norm_back(
            grad_normed_two, normed_two, scale_two, gain_two
        )
        low_resid = grad_resid.astype(jnp.bfloat16)
        grad_attn_rows = gather(low_resid)
        down_total = y_total("down", after(down_y, low_resid))
        down_h = over_h(down_total)
        ffn_from_twin = flip(after(ffn_twin, low_resid), "k")
        (ffn_x, ffn_l), ffn_rest = scatter_first(ffn_own, ffn_from_twin)
        gate_total = y_total("gate", after(gate_y, down_total))
        gate_h = over_h(gate_total)
        up_total = y_total("up", after(up_y, gate_total))
        up_h = over_h(up_total)
        grad_attn_rows, up_total, ffn_x, ffn_l = sync(grad_attn_rows, up_total, ffn_x, ffn_l)

        grad_qkv = attention_back(
            first, place, ends, grad_attn_rows, wo, qkv, ratio, denom
        )
        grad_qkv, down_h, gate_h = sync(grad_qkv, down_h, gate_h)

        from_twin = flip(product_rows(stacked, grad_qkv, w_qkv), "k")
        one_own = product_rows(stacked + 4, grad_qkv, w_qkv)
        (first_x, first_l), rest = scatter_first(one_own, from_twin)
        head_part, head_other, gain_one_part = head_grads(
            after(grad_qkv, first_x),
            stack_twin,
            stack_own,
            mixed_heads,
            grad_attn_rows,
            w_qkv,
            gain_one,
        )
        head_y = over_y(head_other)
        down_total = after(down_total, head_other) + down_h
        down_back = over_owners(down_total)
        got_x, got_l, up_h = sync(flip(first_x, "x"), flip(first_l, "l"), up_h)
        to_x, to_l = scatter_last(got_x, got_l, rest)
        gain_grads = jnp.concatenate([gain_one_part, gain_two_part[None]], axis=0)
        gate_total = after(gate_total, to_x) + gate_h
        gate_back = over_owners(gate_total)
        grad_normed_one = scatter_end(got_x, got_l, flip(to_x, "x"), flip(to_l, "l"), rest)
        grad_normed_one, ffn_x, ffn_l = sync(grad_normed_one, ffn_x, ffn_l)

        grad_tokens = grad_resid + norm_back(grad_normed_one, normed_one, scale_one, gain_one)
        low_tokens = grad_tokens.astype(jnp.bfloat16)
        grad_tokens = trade(low_tokens)
        head_total = all_y((after(head_part, low_tokens) + head_y).astype(jnp.bfloat16))
        head_h = over_h(head_total)
        flags = jnp.stack(
            [lax.axis_index("y") % 2, (lax.axis_index("k") == lax.axis_index("h")).astype(jnp.int32)]
        )

        def spread(total, back):
            return total, to_twin(total), back, to_twin(back)

        down_parts, gate_parts = spread(down_total, down_back), spread(gate_total, gate_back)
        grad_tokens, head_h, up_total, got_x, got_l, *parts = sync(
            grad_tokens,
            head_h,
            up_total,
            flip(ffn_x, "x"),
            flip(ffn_l, "l"),
            *down_parts,
            *gate_parts,
        )
        head_total = head_total + head_h
        head_back, head_cross = over_owners(head_total), across(head_total)
        up_total = up_total + up_h
        up_back = over_owners(up_total)
        to_x, to_l = scatter_last(got_x, got_l, ffn_rest)
        last_x, last_l, down_grad, gate_grad, up_back = sync(
            flip(to_x, "x"),
            flip(to_l, "l"),
            finish_unit(flags, *parts[:4]),
            finish_unit(flags, *parts[4:]),
            up_back,
        )
        ffn_out = scatter_end(got_x, got_l, last_x, last_l, ffn_rest)
        block_out = trade((residual + ffn_out).astype(jnp.bfloat16))
        up_grad = finish_unit(flags, *spread(up_total, up_back))
        query_grad, key_grad, value_grad, out_grad = finish_head(
            flags, head_total, to_twin(head_total), head_back, head_cross
        )
        for name in ("k", "x", "l", "h"):
            gain_grads = gain_grads + flip(gain_grads, name)
        step = 1
        while step < y_size:
            gain_grads = gain_grads + lax.ppermute(
                gain_grads, "y", [(i, i ^ step) for i in range(y_size)]
            )
            step *= 2

        return (
            block_out,
            grad_tokens.astype(jnp.float32),
            gain_grads[0],
            query_grad.T,
            key_grad.T,
            value_grad,
            out_grad,
            gain_grads[1],
            gate_grad.T,
            up_grad.T,
            down_grad,
        )

    return body


def solution(mesh):
    dp_size, tensor_size = mesh.devices.shape
    fine = Mesh(mesh.devices.reshape(dp_size // 2, 2, 2, 2, tensor_size // 4), ALL_AXES)
    rows = P(ALL_AXES, None)
    shard = ("h", "l", "x")
    in_specs = (
        rows,
        P(),
        P(None, shard),
        P(None, shard),
        P(None, shard),
        P(shard, None),
        P(),
        P(None, shard),
        P(None, shard),
        P(shard, None),
        P(("y", "k"), None),
        rows,
    )
    out_specs = (
        rows,
        rows,
        P(),
        P(None, shard),
        P(None, shard),
        P(None, shard),
        P(shard, None),
        P(),
        P(None, shard),
        P(None, shard),
        P(shard, None),
    )
    return jax.shard_map(
        make_body(dp_size // 2), mesh=fine, in_specs=in_specs, out_specs=out_specs, check_vma=False
    )
```

```python
import functools

import jax
import jax.numpy as jnp
from jax import lax
from jax.experimental import pallas as pl
from jax.experimental.pallas import tpu as pltpu
from jax.sharding import Mesh
from jax.sharding import PartitionSpec as P

FEAT = 16
HEAD_V = 128
EPS = 1e-05
VALUES = 2 * HEAD_V
FEATS = 2 * FEAT
NO_COST = pl.CostEstimate(flops=1, bytes_accessed=1, transcendentals=0)

ALL_AXES = ("y", "k", "h", "l", "x")
FLIP = [(0, 1), (1, 0)]
SQUARE = ("k", "l", "x")


def norm_rows(values, gain_vec):
    row_scale = lax.rsqrt(jnp.mean(values * values, axis=-1, keepdims=True) + EPS)
    normed = values * row_scale
    return (normed, row_scale, (normed * gain_vec).astype(jnp.bfloat16))


def norm_back(grad_normed, normed, row_scale, gain_vec):
    weighted = grad_normed * gain_vec
    inner_mean = jnp.mean(weighted * normed, axis=-1, keepdims=True)
    return row_scale * (weighted - normed * inner_mean)


def dot_nn(left_mat, right_mat):
    return jnp.dot(left_mat, right_mat, preferred_element_type=jnp.float32)


def dot_tn(left_mat, right_mat):
    return lax.dot_general(
        left_mat, right_mat, (((0,), (0,)), ((), ())), preferred_element_type=jnp.float32
    )


def dot_nt(left_mat, right_mat):
    return lax.dot_general(
        left_mat, right_mat, (((1,), (1,)), ((), ())), preferred_element_type=jnp.float32
    )


def head_lanes(values, head):
    lane = lax.broadcasted_iota(jnp.int32, values.shape, 1)
    return jnp.where((lane >= head * FEAT) & (lane < (head + 1) * FEAT), values, jnp.zeros_like(values))

def scores(query, keys, ends_ref, i, j, block):
    score = dot_nt(query, keys) * 0.25
    t = i * block + lax.broadcasted_iota(jnp.int32, score.shape, 0)
    u = j * block + lax.broadcasted_iota(jnp.int32, score.shape, 1)
    ends = ends_ref[:, pl.ds(pl.multiple_of(jnp.minimum(j, i) * block, block), block)]
    allowed = (t >= u) & (t <= ends)
    return score, allowed, jnp.where(allowed, 1.0 + score + 0.5 * score * score, 0.0)

def forward_kernel(
    first_ref,
    twin_at_ref,
    own_at_ref,
    is_own_ref,
    twin_ref,
    own_ref,
    weight_ref,
    ends_ref,
    qkv_ref,
    mixed_ref,
    ratio_ref,
    denom_ref,
    key_ref,
    numer_ref,
    sum_ref,
):
    i = pl.program_id(0)
    block = own_ref.shape[0]
    here = pl.ds(pl.multiple_of(i * block, block), block)

    def project(rows_ref):
        qkv_ref[here] = dot_nt(rows_ref[...], weight_ref[...]).astype(jnp.bfloat16)

    pl.when(is_own_ref[i] == 1)(lambda: project(own_ref))
    pl.when(is_own_ref[i] == 0)(lambda: project(twin_ref))
    key_ref[here] = qkv_ref[here, VALUES + FEATS :]
    query = qkv_ref[here, VALUES : VALUES + FEATS]
    own = [head_lanes(query, head) for head in range(2)]
    numer_ref[...] = jnp.zeros_like(numer_ref)
    sum_ref[...] = jnp.zeros_like(sum_ref)

    def step(pair, carry):
        for head in range(2):
            columns = pl.ds(head * HEAD_V, HEAD_V)
            folded, numer = None, None
            for j in (first_ref[i] + 2 * pair, first_ref[i] + 2 * pair + 1):
                there = pl.ds(pl.multiple_of(jnp.minimum(j, i) * block, block), block)
                _, _, kernel = scores(own[head], key_ref[there], ends_ref, i, j, block)
                parts = [kernel[:, c * 128 : (c + 1) * 128] for c in range(block // 128)]
                part = dot_nn(kernel.astype(jnp.bfloat16), qkv_ref[there, columns])
                folded = sum(parts) if folded is None else folded + sum(parts)
                numer = part if numer is None else numer + part
            sum_ref[:, pl.ds(head * 128, 128)] += folded
            numer_ref[:, columns] += numer
        return carry

    lax.fori_loop(0, (i + 2 - first_ref[i]) // 2, step, 0)
    for head in range(2):
        columns = pl.ds(head * HEAD_V, HEAD_V)
        denom = jnp.sum(sum_ref[:, pl.ds(head * 128, 128)], axis=1, keepdims=True)
        ratio = numer_ref[:, columns] / denom
        mixed_ref[:, columns] = ratio.astype(jnp.bfloat16)
        ratio_ref[:, columns] = ratio
        denom_ref[:, columns] = jnp.broadcast_to(denom, ratio.shape)

def attention_rows(first, places, ends, twin, own, weight):
    half_rows, model = own.shape
    group_rows = 2 * half_rows
    block = group_rows // 8
    width = VALUES + 2 * FEATS

    def by_rows(columns):
        return pl.BlockSpec((block, columns), lambda i, *_: (i, 0))

    def whole(shape):
        return pl.BlockSpec(shape, lambda i, *_: (0, 0))

    return pl.pallas_call(
        forward_kernel,
        out_shape=[
            jax.ShapeDtypeStruct((group_rows, width), jnp.bfloat16),
            jax.ShapeDtypeStruct((group_rows, VALUES), jnp.bfloat16),
            jax.ShapeDtypeStruct((group_rows, VALUES), jnp.float32),
            jax.ShapeDtypeStruct((group_rows, VALUES), jnp.float32),
        ],
        grid_spec=pltpu.PrefetchScalarGridSpec(
            num_scalar_prefetch=4,
            grid=(8,),
            in_specs=[
                pl.BlockSpec((block, model), lambda i, f, twin_at, own_at, s: (twin_at[i], 0)),
                pl.BlockSpec((block, model), lambda i, f, twin_at, own_at, s: (own_at[i], 0)),
                whole((width, model)),
                whole((1, group_rows)),
            ],
            out_specs=[
                whole((group_rows, width)),
                by_rows(VALUES),
                by_rows(VALUES),
                by_rows(VALUES),
            ],
            scratch_shapes=[
                pltpu.VMEM((group_rows, FEATS), jnp.bfloat16),
                pltpu.VMEM((block, VALUES), jnp.float32),
                pltpu.VMEM((block, 256), jnp.float32),
            ],
        ),
        compiler_params=pltpu.CompilerParams(vmem_limit_bytes=32 << 20),
        cost_estimate=NO_COST,
        name="attention_rows",
    )(first, *places, twin, own, weight, ends)


def backward_kernel(
    first_ref,
    place_ref,
    attn_ref,
    weight_ref,
    qkv_ref,
    ratio_ref,
    denom_ref,
    ends_ref,
    grad_ref,
    key_ref,
    key_sum,
    value_sum,
    query_sum,
):
    i = pl.program_id(0)
    block = attn_ref.shape[0]
    here = pl.ds(pl.multiple_of(i * block, block), block)
    @pl.when(i == 0)
    def _():
        key_ref[...] = qkv_ref[:, VALUES + FEATS:]
        key_sum[...] = jnp.zeros_like(key_sum)
        value_sum[...] = jnp.zeros_like(value_sum)
    mixed_grad = dot_nt(attn_ref[...], weight_ref[...]).astype(jnp.bfloat16).astype(jnp.float32)
    query = qkv_ref[here, VALUES : VALUES + FEATS]
    own = [head_lanes(query, head) for head in range(2)]
    numer_grads, denom_grads = [], []
    for head in range(2):
        columns = pl.ds(head * HEAD_V, HEAD_V)
        grad = mixed_grad[:, head * HEAD_V : (head + 1) * HEAD_V]
        denom = denom_ref[:, columns]
        numer_grads.append((grad / denom).astype(jnp.bfloat16))
        denom_grads.append(-jnp.sum(grad * ratio_ref[:, columns], axis=1, keepdims=True) / denom[:, :1])
    query_sum[...] = jnp.zeros_like(query_sum)

    def step(j, carry):
        there = pl.ds(pl.multiple_of(j * block, block), block)
        keys = key_ref[there]
        key_grads = None
        for head in range(2):
            columns = pl.ds(head * HEAD_V, HEAD_V)
            score, allowed, kernel = scores(own[head], keys, ends_ref, i, j, block)
            kernel_grad = dot_nt(numer_grads[head], qkv_ref[there, columns]) + denom_grads[head]
            score_grad = jnp.where(allowed, kernel_grad * (1.0 + score), 0.0).astype(jnp.bfloat16)
            query_sum[:, pl.ds(head * 128, FEATS)] += dot_nn(score_grad, keys)
            key_grad = dot_tn(score_grad, own[head])
            key_grads = key_grad if key_grads is None else key_grads + key_grad
            value_sum[there, columns] += dot_tn(kernel.astype(jnp.bfloat16), numer_grads[head])
        key_sum[there] += key_grads
        return carry

    lax.fori_loop(first_ref[i], i + 1, step, 0)
    totals = [query_sum[:, pl.ds(head * 128, FEATS)] for head in range(2)]
    query_grad = (head_lanes(totals[0], 0) + head_lanes(totals[1], 1)) * 0.25
    placed = pl.ds(pl.multiple_of(place_ref[i] * block, block), block)
    grad_ref[placed, VALUES : VALUES + FEATS] = query_grad.astype(jnp.bfloat16)

    @pl.when(i == pl.num_programs(0) - 1)
    def _():
        def store(j, carry):
            there = pl.ds(pl.multiple_of(j * block, block), block)
            placed = pl.ds(pl.multiple_of(place_ref[j] * block, block), block)
            grad_ref[placed, :VALUES] = value_sum[there].astype(jnp.bfloat16)
            grad_ref[placed, VALUES + FEATS :] = (key_sum[there] * 0.25).astype(jnp.bfloat16)
            return carry

        lax.fori_loop(0, pl.num_programs(0), store, 0)

def attention_back(first, place, ends, attn_rows, weight, qkv, ratio, denom):
    group_rows, model = attn_rows.shape
    block = group_rows // 8
    width = VALUES + 2 * FEATS

    def by_rows(columns):
        return pl.BlockSpec((block, columns), lambda i, *_: (i, 0))

    def whole(shape):
        return pl.BlockSpec(shape, lambda i, *_: (0, 0))

    return pl.pallas_call(
        backward_kernel,
        out_shape=jax.ShapeDtypeStruct((group_rows, width), jnp.bfloat16),
        grid_spec=pltpu.PrefetchScalarGridSpec(
            num_scalar_prefetch=2,
            grid=(8,),
            in_specs=[
                by_rows(model),
                whole((VALUES, model)),
                whole((group_rows, width)),
                by_rows(VALUES),
                by_rows(VALUES),
                whole((1, group_rows)),
            ],
            out_specs=whole((group_rows, width)),
            scratch_shapes=[
                pltpu.VMEM((group_rows, FEATS), jnp.bfloat16),
                pltpu.VMEM((group_rows, FEATS), jnp.float32),
                pltpu.VMEM((group_rows, VALUES), jnp.float32),
                pltpu.VMEM((block, 256), jnp.float32),
            ],
        ),
        compiler_params=pltpu.CompilerParams(vmem_limit_bytes=40 << 20),
        cost_estimate=NO_COST,
        name="attention_back",
    )(first, place, attn_rows, weight, qkv, ratio, denom, ends)


def bounds(doc_row):
    group_rows = doc_row.shape[0]; block = group_rows // 8
    ends = jnp.sum(doc_row[:, None] <= doc_row[None, :], axis=0, dtype=jnp.int32) - 1
    starts = block * jnp.arange(8, dtype=jnp.int32)
    first = jnp.sum(ends[block - 1 :: block][None, :] < starts[:, None], axis=1, dtype=jnp.int32)
    return first, ends.reshape(1, group_rows)


def ffn_kernel(pieces, order_ref, rows_ref, grad_ref, *refs):
    weights = refs[:4]
    act_grad_ref, hidden_ref, part_ref, held, sems = refs[-5:]

    @pl.when(pl.program_id(0) == 0)
    def _():
        copies = [
            pltpu.make_async_copy(ref, held.at[pl.ds(i * pieces, pieces)], sems.at[i])
            for i, ref in enumerate(weights)
        ]
        for copy in copies:
            copy.start()

    rows = rows_ref[...]
    for half in range(2):
        at = 2 * half * pieces

        @pl.when(pl.program_id(0) == 0)
        def _(half=half):
            for i in (2 * half, 2 * half + 1):
                pltpu.make_async_copy(
                    weights[i], held.at[pl.ds(i * pieces, pieces)], sems.at[i]
                ).wait()

        gate = dot_nt(held[pl.ds(at, pieces)], rows)
        up = dot_nt(held[pl.ds(at + pieces, pieces)], rows)
        grad = grad_ref[pl.ds(half * pieces, pieces)]
        sigmoid = jax.nn.sigmoid(gate)
        act = gate * sigmoid
        hidden_ref[pl.ds(half * pieces, pieces)] = (act * up).astype(jnp.bfloat16)
        act_grad_ref[pl.ds(at, pieces)] = (
            grad * up * (sigmoid * (1.0 + gate * (1.0 - sigmoid)))
        ).astype(jnp.bfloat16)
        act_grad_ref[pl.ds(at + pieces, pieces)] = (grad * act).astype(jnp.bfloat16)
    part_ref[...] = dot_tn(act_grad_ref[...], held[...]).astype(jnp.bfloat16)


def ffn_rows(order, rows, grad_hidden, weights, earlier=()):
    group_rows, model = rows.shape
    pieces = weights[0].shape[0]
    block = group_rows // 8
    blocks = order.shape[0]
    anywhere = pl.BlockSpec(memory_space=pl.ANY)
    return pl.pallas_call(
        functools.partial(ffn_kernel, pieces),
        out_shape=[
            jax.ShapeDtypeStruct((4 * pieces, group_rows), jnp.bfloat16),
            jax.ShapeDtypeStruct((2 * pieces, group_rows), jnp.bfloat16),
            jax.ShapeDtypeStruct((blocks * block, model), jnp.bfloat16),
        ],
        grid_spec=pltpu.PrefetchScalarGridSpec(
            num_scalar_prefetch=1,
            grid=(blocks,),
            in_specs=[
                pl.BlockSpec((block, model), lambda i, o: (o[i], 0)),
                pl.BlockSpec((2 * pieces, block), lambda i, o: (0, o[i])),
                *[anywhere] * (4 + len(earlier)),
            ],
            out_specs=[
                pl.BlockSpec((4 * pieces, block), lambda i, o: (0, o[i])),
                pl.BlockSpec((2 * pieces, block), lambda i, o: (0, o[i])),
                pl.BlockSpec((block, model), lambda i, o: (i, 0)),
            ],
            scratch_shapes=[
                pltpu.VMEM((4 * pieces, model), jnp.bfloat16),
                pltpu.SemaphoreType.DMA((4,)),
            ],
        ),
        input_output_aliases={7 + i: i for i in range(len(earlier))},
        compiler_params=pltpu.CompilerParams(vmem_limit_bytes=44 << 20),
        cost_estimate=NO_COST,
        name="ffn_rows",
    )(order, rows, grad_hidden, *weights, *earlier)


def product_kernel(turned, order_ref, rows_ref, weight_ref, part_ref):
    product = dot_tn if turned else dot_nn
    part_ref[...] = product(rows_ref[...], weight_ref[...]).astype(jnp.bfloat16)


def product_rows(order, rows, weight, turned=False):
    group_rows = rows.shape[1 if turned else 0]
    depth, model = weight.shape
    block = group_rows // 8
    blocks = order.shape[0]
    if turned:
        rows_spec = pl.BlockSpec((depth, block), lambda i, o: (0, o[i]))
    else:
        rows_spec = pl.BlockSpec((block, depth), lambda i, o: (o[i], 0))
    return pl.pallas_call(
        functools.partial(product_kernel, turned),
        out_shape=jax.ShapeDtypeStruct((blocks * block, model), jnp.bfloat16),
        grid_spec=pltpu.PrefetchScalarGridSpec(
            num_scalar_prefetch=1,
            grid=(blocks,),
            in_specs=[rows_spec, pl.BlockSpec((depth, model), lambda i, o: (0, 0))],
            out_specs=pl.BlockSpec((block, model), lambda i, o: (i, 0)),
        ),
        compiler_params=pltpu.CompilerParams(vmem_limit_bytes=24 << 20),
        cost_estimate=NO_COST,
        name="product_rows",
    )(order, rows, weight)


def unit_kernel(with_arrived, acts_ref, rows_ref, *refs):
    total = dot_nn(acts_ref[...], rows_ref[...])
    if with_arrived:
        total = total + refs[0][...]
    refs[-1][...] = total.astype(jnp.bfloat16)


def unit_grad(acts, piece, pieces, rows, arrived=None):
    units = acts.shape[0] // pieces
    group_rows, model = rows.shape
    columns = model // 4
    part = pl.BlockSpec((units, columns), lambda i: (0, i))
    return pl.pallas_call(
        functools.partial(unit_kernel, arrived is not None),
        out_shape=jax.ShapeDtypeStruct((units, model), jnp.bfloat16),
        grid=(4,),
        in_specs=[
            pl.BlockSpec((units, group_rows), lambda i: (piece, 0)),
            pl.BlockSpec((group_rows, columns), lambda i: (0, i)),
            *([] if arrived is None else [part]),
        ],
        out_specs=part,
        compiler_params=pltpu.CompilerParams(vmem_limit_bytes=24 << 20),
        cost_estimate=NO_COST,
        name="unit_grad",
    )(acts, rows, *([] if arrived is None else [arrived]))


def hidden_kernel(mine_ref, other_ref, rows_ref, grad_ref):
    half = mine_ref.shape[0]
    grad_ref[pl.ds(0, half)] = dot_nt(mine_ref[...], rows_ref[...])
    grad_ref[pl.ds(half, half)] = dot_nt(other_ref[...], rows_ref[...])


def hidden_grad(mine, other, rows):
    half, model = mine.shape
    group_rows = rows.shape[0]
    block = group_rows // 4
    weight = pl.BlockSpec((half, model), lambda i: (0, 0))
    return pl.pallas_call(
        hidden_kernel,
        out_shape=jax.ShapeDtypeStruct((2 * half, group_rows), jnp.float32),
        grid=(4,),
        in_specs=[weight, weight, pl.BlockSpec((block, model), lambda i: (i, 0))],
        out_specs=pl.BlockSpec((2 * half, block), lambda i: (0, i)),
        compiler_params=pltpu.CompilerParams(vmem_limit_bytes=28 << 20),
        cost_estimate=NO_COST,
        name="hidden_grad",
    )(mine, other, rows)


def head_kernel(
    qkv_ref, twin_ref, own_ref, mixed_ref, attn_ref, weight_ref, gain_ref, mine_ref, other_ref, sum_ref
):
    half = twin_ref.shape[0]
    qkv = dot_tn(qkv_ref[pl.ds(0, half)], twin_ref[...]) + dot_tn(
        qkv_ref[pl.ds(half, half)], own_ref[...]
    )
    out = dot_tn(mixed_ref[...], attn_ref[...])
    gain_grad = jnp.sum(qkv * weight_ref[...].astype(jnp.float32), axis=0, keepdims=True)
    sum_ref[...] = gain_grad / gain_ref[...]
    for which, ref in enumerate((mine_ref, other_ref)):
        at = VALUES + which * FEAT
        ref[pl.ds(0, HEAD_V)] = qkv[which * HEAD_V : (which + 1) * HEAD_V].astype(ref.dtype)
        ref[pl.ds(HEAD_V, FEAT)] = qkv[at : at + FEAT].astype(ref.dtype)
        ref[pl.ds(HEAD_V + FEAT, FEAT)] = qkv[at + FEATS : at + FEATS + FEAT].astype(ref.dtype)
        ref[pl.ds(HEAD_V + 2 * FEAT, HEAD_V)] = out[which * HEAD_V : (which + 1) * HEAD_V].astype(
            ref.dtype
        )


def head_grads(qkv, twin, own, mixed, attn_rows, weight, gain):
    group_rows, model = attn_rows.shape
    columns = model // 4
    size = 2 * HEAD_V + 2 * FEAT

    def whole(values):
        return pl.BlockSpec(values.shape, lambda i: (0, 0))

    def part(rows):
        return pl.BlockSpec((rows, columns), lambda i: (0, i))

    return pl.pallas_call(
        head_kernel,
        out_shape=[
            jax.ShapeDtypeStruct((size, model), jnp.float32),
            jax.ShapeDtypeStruct((size, model), jnp.bfloat16),
            jax.ShapeDtypeStruct((1, model), jnp.float32),
        ],
        grid=(4,),
        in_specs=[
            whole(qkv),
            part(group_rows // 2),
            part(group_rows // 2),
            whole(mixed),
            part(group_rows),
            part(weight.shape[0]),
            part(1),
        ],
        out_specs=[part(size), part(size), part(1)],
        compiler_params=pltpu.CompilerParams(vmem_limit_bytes=32 << 20),
        cost_estimate=NO_COST,
        name="head_grads",
    )(qkv, twin, own, mixed, attn_rows, weight, gain.reshape(1, model))


def chosen(flags_ref, own_ref, twin_ref):
    return jnp.where(flags_ref[1] == 1, own_ref[...], twin_ref[...]).astype(jnp.float32)


def finish_kernel(flags_ref, mine_ref, mine_twin_ref, theirs_ref, theirs_twin_ref, grad_ref):
    half = mine_ref.shape[0]
    mine, theirs = pl.ds(flags_ref[0] * half, half), pl.ds((1 - flags_ref[0]) * half, half)
    grad_ref[mine] = chosen(flags_ref, mine_ref, mine_twin_ref)
    grad_ref[theirs] = chosen(flags_ref, theirs_ref, theirs_twin_ref)


def finish_unit(flags, *parts):
    half, model = parts[0].shape
    columns = model // 4
    part = pl.BlockSpec((half, columns), lambda i, f: (0, i))
    return pl.pallas_call(
        finish_kernel,
        out_shape=jax.ShapeDtypeStruct((2 * half, model), jnp.float32),
        grid_spec=pltpu.PrefetchScalarGridSpec(
            num_scalar_prefetch=1,
            grid=(4,),
            in_specs=[part] * 4,
            out_specs=pl.BlockSpec((2 * half, columns), lambda i, f: (0, i)),
        ),
        compiler_params=pltpu.CompilerParams(vmem_limit_bytes=24 << 20),
        cost_estimate=NO_COST,
        name="finish_unit",
    )(flags, *parts)


def finish_head_kernel(
    flags_ref, mine_ref, mine_twin_ref, theirs_ref, theirs_twin_ref, query_ref, key_ref, value_ref, out_ref
):
    halves = (
        (flags_ref[0], chosen(flags_ref, mine_ref, mine_twin_ref)),
        (1 - flags_ref[0], chosen(flags_ref, theirs_ref, theirs_twin_ref)),
    )
    for at, grads in halves:
        features = pl.ds(pl.multiple_of(at * FEAT, FEAT), FEAT)
        values = pl.ds(pl.multiple_of(at * HEAD_V, HEAD_V), HEAD_V)
        value_ref[:, values] = grads[:HEAD_V].T
        query_ref[features] = grads[HEAD_V : HEAD_V + FEAT]
        key_ref[features] = grads[HEAD_V + FEAT : HEAD_V + 2 * FEAT]
        out_ref[values] = grads[HEAD_V + 2 * FEAT :]


def finish_head(flags, *parts):
    size, model = parts[0].shape
    columns = model // 4

    def part(rows):
        return pl.BlockSpec((rows, columns), lambda i, f: (0, i))

    return pl.pallas_call(
        finish_head_kernel,
        out_shape=[
            jax.ShapeDtypeStruct((FEATS, model), jnp.float32),
            jax.ShapeDtypeStruct((FEATS, model), jnp.float32),
            jax.ShapeDtypeStruct((model, VALUES), jnp.float32),
            jax.ShapeDtypeStruct((VALUES, model), jnp.float32),
        ],
        grid_spec=pltpu.PrefetchScalarGridSpec(
            num_scalar_prefetch=1,
            grid=(4,),
            in_specs=[part(size)] * 4,
            out_specs=[
                part(FEATS),
                part(FEATS),
                pl.BlockSpec((columns, VALUES), lambda i, f: (i, 0)),
                part(VALUES),
            ],
        ),
        compiler_params=pltpu.CompilerParams(vmem_limit_bytes=24 << 20),
        cost_estimate=NO_COST,
        name="finish_head",
    )(flags, *parts)


def sync(*values):
    return lax.optimization_barrier(values)


def after(value, *others):
    return lax.optimization_barrier((value, *others))[0]


def make_body(y_size):
    y_pairs = [(i, i ^ 1) for i in range(y_size)]
    owner_y_pairs = [(i * 4 + kh, (i ^ 1) * 4 + kh) for i in range(y_size) for kh in (0, 3)]

    cross_pairs = [(i * 4 + kh, (i ^ 1) * 4 + (kh ^ 2)) for i in range(y_size) for kh in (0, 3)]

    def trade(values):
        return lax.ppermute(values, ("k", "h"), [(0, 0), (1, 2), (2, 1), (3, 3)])

    def over_y(values):
        return lax.ppermute(values, "y", y_pairs)

    def over_h(values):
        return lax.ppermute(values, ("k", "h"), [(1, 0), (2, 3)])

    def over_owners(values):
        return lax.ppermute(values, ("y", "k", "h"), owner_y_pairs)

    def to_twin(values):
        return lax.ppermute(values, ("k", "h"), [(0, 2), (3, 1)])

    def across(values):
        return lax.ppermute(values, ("y", "k", "h"), cross_pairs)

    def all_y(total):
        step = 2
        while step < y_size:
            total = total + lax.ppermute(total, "y", [(i, i ^ step) for i in range(y_size)])
            step *= 2
        return total

    def my_half(own, axis=0):
        half = own.shape[axis] // 2
        return lax.dynamic_slice_in_dim(own, (lax.axis_index("y") % 2) * half, half, axis)

    def orders():
        k, l, x = (lax.axis_index(name) for name in SQUARE)
        chips = jnp.array([3, 1, 2, 0], jnp.int32) ^ (2 * l + x)
        return (chips + 4 * (1 - k), chips + 4 * k)

    def places():
        k, l, x = (lax.axis_index(name) for name in SQUARE)
        index = jnp.arange(8, dtype=jnp.int32)

        def slot(block):
            chip = (block % 4) ^ (2 * l + x)
            return jnp.where((chip == 0) | (chip == 3), 3 - chip, chip)

        first_twin = 4 * (1 - k)
        twin_at = slot(jnp.clip(index, first_twin, first_twin + 3))
        own_at = slot(jnp.clip(index, 4 * k, 4 * k + 3))
        is_own = (index // 4 == k).astype(jnp.int32)
        return (twin_at, own_at, is_own), slot(index) + 4 * is_own

    def low(*values):
        return jnp.concatenate(values, axis=0).astype(jnp.bfloat16)

    def scatter_first(mine, from_twin):
        rows = mine.shape[0] // 4
        half = rows // 2

        def chip(start, stop):
            return mine[start:stop].astype(jnp.float32) + from_twin[start:stop]

        first_x = low(chip(0, half), chip(rows, rows + half))
        first_l = low(chip(half, rows), chip(2 * rows + half, 3 * rows))
        rest = (
            chip(rows + half, 2 * rows),
            chip(2 * rows, 2 * rows + half),
            chip(3 * rows, 4 * rows),
        )
        return sync(first_x, first_l), rest

    def scatter_last(got_x, got_l, rest):
        half = got_x.shape[0] // 2
        return sync(low(rest[0] + got_l[:half]), low(rest[1] + got_x[:half]))

    def scatter_end(got_x, got_l, last_x, last_l, rest):
        half = got_x.shape[0] // 2
        own_top = rest[2][:half] + got_x[half:] + last_l
        own_bottom = rest[2][half:] + last_x + got_l[half:]
        return jnp.concatenate([own_top, own_bottom], axis=0)

    def flip(values, name):
        return lax.ppermute(values, name, FLIP)

    def gather(rows):
        return lax.all_gather(rows, SQUARE, axis=0, tiled=True)

    def low_dot(left, right):
        return dot_nn(left, right).astype(jnp.bfloat16)

    def body(
        tokens,
        gain_one,
        w_query,
        w_key,
        w_value,
        w_out,
        gain_two,
        w_gate,
        w_up,
        w_down,
        doc_ids,
        cotangent,
    ):
        for_twin, for_own = orders()
        halves_at, place = places()
        stacked = jnp.arange(4, dtype=jnp.int32)
        qkv_size = HEAD_V + 2 * FEAT
        head_size = qkv_size + HEAD_V
        own_tokens = trade(tokens)
        head_half = jnp.concatenate(
            [
                my_half(w_value, 1).T,
                my_half(w_query.T),
                my_half(w_key.T),
                my_half(w_out),
                jnp.broadcast_to(doc_ids.astype(jnp.bfloat16), (16, doc_ids.shape[1])),
            ],
            axis=0,
        )
        down_half, gate_half, up_half = my_half(w_down), my_half(w_gate.T), my_half(w_up.T)
        own_tokens = after(own_tokens, head_half, down_half, gate_half, up_half)
        inputs = own_tokens.astype(jnp.float32)
        normed_one, scale_one, low_one = norm_rows(inputs, gain_one)

        head_mine = trade(after(head_half, low_one))
        from_x, from_l, head_mine, own_grad = sync(
            flip(low_one, "x"), flip(low_one, "l"), head_mine, trade(after(cotangent, low_one))
        )
        grad_rows = gather(own_grad)
        half = low_one.shape[0] // 2
        qkv_other = over_y(head_mine[:qkv_size])
        d_top = flip(from_l[:half], "x")
        d_bottom = flip(from_x[half:], "l")
        stack_own = jnp.concatenate([d_top, d_bottom, from_x, from_l, low_one], axis=0)
        stack_own, qkv_other = sync(stack_own, qkv_other)
        stack_twin = flip(stack_own, "k")
        wo_other = over_y(after(head_mine[qkv_size:head_size], qkv_other))
        first, ends = bounds(head_mine[head_size].astype(jnp.int32))
        w_qkv = jnp.concatenate(
            [
                head_mine[:HEAD_V],
                qkv_other[:HEAD_V],
                head_mine[HEAD_V : HEAD_V + FEAT],
                qkv_other[HEAD_V : HEAD_V + FEAT],
                head_mine[HEAD_V + FEAT : qkv_size],
                qkv_other[HEAD_V + FEAT : qkv_size],
            ],
            axis=0,
        )
        stack_twin, w_qkv, first = sync(stack_twin, w_qkv, first)

        down_mine = trade(after(down_half, own_grad))
        qkv, mixed_heads, ratio, denom = attention_rows(
            first, halves_at, ends, stack_twin, stack_own, w_qkv
        )
        mixed_heads, wo_other = sync(mixed_heads, wo_other)
        wo = jnp.concatenate([head_mine[qkv_size:head_size], wo_other], axis=0)

        from_twin = flip(product_rows(for_twin, mixed_heads, wo), "k")
        from_twin, down_mine = sync(from_twin, down_mine)
        down_other = over_y(down_mine)
        gate_mine = trade(after(gate_half, down_mine))
        (first_x, first_l), rest = scatter_first(
            product_rows(for_own, mixed_heads, wo), from_twin
        )
        got_x, got_l, down_other = sync(flip(first_x, "x"), flip(first_l, "l"), down_other)
        to_x, to_l = scatter_last(got_x, got_l, rest)
        attn_out = scatter_end(got_x, got_l, flip(to_x, "x"), flip(to_l, "l"), rest)
        attn_out, gate_mine = sync(attn_out, gate_mine)
        up_mine = trade(after(up_half, gate_mine))
        gate_other = over_y(gate_mine)

        residual = inputs + attn_out
        normed_two, scale_two, low_two = norm_rows(residual, gain_two)
        gathered_two = gather(low_two)
        wd = jnp.concatenate([down_mine, down_other], axis=0)
        grad_hidden = hidden_grad(down_mine, down_other, after(grad_rows, low_two, up_mine))
        up_other = over_y(up_mine)
        gathered_two, up_other, gate_other, grad_hidden = sync(
            gathered_two, up_other, gate_other, grad_hidden
        )

        weights = (gate_mine, up_mine, gate_other, up_other)
        *acts, parts_twin = ffn_rows(for_twin, gathered_two, grad_hidden, weights)
        from_twin = flip(parts_twin, "k")
        act_grad, hidden, parts_own = ffn_rows(
            for_own, gathered_two, grad_hidden, weights, tuple(acts)
        )
        unit_rows = {"gate": gathered_two, "up": gathered_two, "down": grad_rows}
        unit_at = {"gate": (0, 2, 4), "up": (1, 3, 4), "down": (0, 1, 2)}

        def other_part(name, *deps):
            _, piece, pieces = unit_at[name]
            acts = after(hidden if pieces == 2 else act_grad, *deps)
            return unit_grad(acts, piece, pieces, unit_rows[name])

        def y_total(name, arrived):
            piece, _, pieces = unit_at[name]
            acts = hidden if pieces == 2 else act_grad
            return all_y(unit_grad(acts, piece, pieces, unit_rows[name], arrived))

        (first_x, first_l), rest = scatter_first(parts_own, from_twin)
        down_part = other_part("down", first_x)
        down_y = over_y(down_part)
        gate_part = other_part("gate", down_part)
        up_part = other_part("up", gate_part)
        got_x, got_l, gate_part, up_part = sync(
            flip(first_x, "x"), flip(first_l, "l"), gate_part, up_part
        )
        to_x, to_l = scatter_last(got_x, got_l, rest)
        late_hidden = after(hidden, to_x)
        ffn_twin = product_rows(for_twin, late_hidden, wd, turned=True)
        ffn_own = product_rows(for_own, late_hidden, wd, turned=True)
        grad_normed_two = scatter_end(got_x, got_l, flip(to_x, "x"), flip(to_l, "l"), rest)
        grad_normed_two, down_y, ffn_twin, ffn_own = sync(
            grad_normed_two, down_y, ffn_twin, ffn_own
        )

        gate_y = over_y(gate_part)
        up_y = over_y(up_part)
        gain_two_part = jnp.sum(grad_normed_two * normed_two, axis=0)
        grad_resid = own_grad.astype(jnp.float32) + norm_back(
            grad_normed_two, normed_two, scale_two, gain_two
        )
        low_resid = grad_resid.astype(jnp.bfloat16)
        grad_attn_rows = gather(low_resid)
        down_total = y_total("down", after(down_y, low_resid))
        down_h = over_h(down_total)
        ffn_from_twin = flip(after(ffn_twin, low_resid), "k")
        (ffn_x, ffn_l), ffn_rest = scatter_first(ffn_own, ffn_from_twin)
        gate_total = y_total("gate", after(gate_y, down_total))
        gate_h = over_h(gate_total)
        up_total = y_total("up", after(up_y, gate_total))
        up_h = over_h(up_total)
        grad_attn_rows, up_total, ffn_x, ffn_l = sync(grad_attn_rows, up_total, ffn_x, ffn_l)

        grad_qkv = attention_back(
            first, place, ends, grad_attn_rows, wo, qkv, ratio, denom
        )
        grad_qkv, down_h, gate_h = sync(grad_qkv, down_h, gate_h)

        from_twin = flip(product_rows(stacked, grad_qkv, w_qkv), "k")
        one_own = product_rows(stacked + 4, grad_qkv, w_qkv)
        (first_x, first_l), rest = scatter_first(one_own, from_twin)
        head_part, head_other, gain_one_part = head_grads(
            after(grad_qkv, first_x),
            stack_twin,
            stack_own,
            mixed_heads,
            grad_attn_rows,
            w_qkv,
            gain_one,
        )
        head_y = over_y(head_other)
        down_total = after(down_total, head_other) + down_h
        down_back = over_owners(down_total)
        got_x, got_l, up_h = sync(flip(first_x, "x"), flip(first_l, "l"), up_h)
        to_x, to_l = scatter_last(got_x, got_l, rest)
        gain_grads = jnp.concatenate([gain_one_part, gain_two_part[None]], axis=0)
        gate_total = after(gate_total, to_x) + gate_h
        gate_back = over_owners(gate_total)
        grad_normed_one = scatter_end(got_x, got_l, flip(to_x, "x"), flip(to_l, "l"), rest)
        grad_normed_one, ffn_x, ffn_l = sync(grad_normed_one, ffn_x, ffn_l)

        grad_tokens = grad_resid + norm_back(grad_normed_one, normed_one, scale_one, gain_one)
        low_tokens = grad_tokens.astype(jnp.bfloat16)
        grad_tokens = trade(low_tokens)
        head_total = all_y((after(head_part, low_tokens) + head_y).astype(jnp.bfloat16))
        head_h = over_h(head_total)
        flags = jnp.stack(
            [lax.axis_index("y") % 2, (lax.axis_index("k") == lax.axis_index("h")).astype(jnp.int32)]
        )

        def spread(total, back):
            return total, to_twin(total), back, to_twin(back)

        down_parts, gate_parts = spread(down_total, down_back), spread(gate_total, gate_back)
        grad_tokens, head_h, up_total, got_x, got_l, *parts = sync(
            grad_tokens,
            head_h,
            up_total,
            flip(ffn_x, "x"),
            flip(ffn_l, "l"),
            *down_parts,
            *gate_parts,
        )
        head_total = head_total + head_h
        head_back, head_cross = over_owners(head_total), across(head_total)
        up_total = up_total + up_h
        up_back = over_owners(up_total)
        to_x, to_l = scatter_last(got_x, got_l, ffn_rest)
        last_x, last_l, down_grad, gate_grad, up_back = sync(
            flip(to_x, "x"),
            flip(to_l, "l"),
            finish_unit(flags, *parts[:4]),
            finish_unit(flags, *parts[4:]),
            up_back,
        )
        ffn_out = scatter_end(got_x, got_l, last_x, last_l, ffn_rest)
        block_out = trade((residual + ffn_out).astype(jnp.bfloat16))
        up_grad = finish_unit(flags, *spread(up_total, up_back))
        query_grad, key_grad, value_grad, out_grad = finish_head(
            flags, head_total, to_twin(head_total), head_back, head_cross
        )
        for name in ("k", "x", "l", "h"):
            gain_grads = gain_grads + flip(gain_grads, name)
        step = 1
        while step < y_size:
            gain_grads = gain_grads + lax.ppermute(
                gain_grads, "y", [(i, i ^ step) for i in range(y_size)]
            )
            step *= 2

        return (
            block_out,
            grad_tokens.astype(jnp.float32),
            gain_grads[0],
            query_grad.T,
            key_grad.T,
            value_grad,
            out_grad,
            gain_grads[1],
            gate_grad.T,
            up_grad.T,
            down_grad,
        )

    return body


def solution(mesh):
    dp_size, tensor_size = mesh.devices.shape
    fine = Mesh(mesh.devices.reshape(dp_size // 2, 2, 2, 2, tensor_size // 4), ALL_AXES)
    rows = P(ALL_AXES, None)
    shard = ("h", "l", "x")
    in_specs = (
        rows,
        P(),
        P(None, shard),
        P(None, shard),
        P(None, shard),
        P(shard, None),
        P(),
        P(None, shard),
        P(None, shard),
        P(shard, None),
        P(("y", "k"), None),
        rows,
    )
    out_specs = (
        rows,
        rows,
        P(),
        P(None, shard),
        P(None, shard),
        P(None, shard),
        P(shard, None),
        P(),
        P(None, shard),
        P(None, shard),
        P(shard, None),
    )
    return jax.shard_map(
        make_body(dp_size // 2), mesh=fine, in_specs=in_specs, out_specs=out_specs, check_vma=False
    )
```
